512 devices in a mesh: wide: 64 (over y, x, core), narrow: 8 (over z).
Axes of the slice: x: 4, y: 8, z: 8, core: 2. Of those that a mesh axis runs over, the one named last changes fastest.
Arguments:
- patches: bfloat16 [64, 256, 1280], P('wide', None, 'narrow'), may hold values from -8 to 8
- grid: int32 [64, 2], P('wide'), may hold values from 2 to 16, as said below
- vit_gain: float32 [1280], replicated, may hold values from 0.25 to 1.75
- vit_qkv: bfloat16 [1280, 3840], P('wide', 'narrow'), may hold values from -1 to 1
- vit_out: bfloat16 [1280, 1280], P('narrow', 'wide'), may hold values from -0.625 to 0.625
- merge_weight: bfloat16 [4, 1280, 1280], P(None, 'narrow', 'wide'), may hold values from -0.078125 to 0.078125
- text_embeds: bfloat16 [10240, 1280], P('wide', 'narrow'), may hold values from -8 to 8
- prompt_pos: int32 [64, 64], replicated, may hold values from -1 to 10239, as said below
- dec_gain: float32 [1280], replicated, may hold values from 0.25 to 1.75
- dec_qkv: bfloat16 [1280, 3840], P('wide', 'narrow'), may hold values from -1 to 1
- dec_out: bfloat16 [1280, 1280], P('narrow', 'wide'), may hold values from -1.25 to 1.25
Outputs:
- decoded: bfloat16 [10240, 1280], P('wide', 'narrow')
The draws below stay inside these ranges and needn't reach their ends.
Inputs may be any that keep to these rules, and one draw needn't show every extreme that they name: `prompt_pos`: grid entries are even; a merged slot (r, c) is live when 2r < grid rows and 2c < grid columns; live slots carry distinct positions, one image's live slots being consecutive in row-major order, and padded slots carry -1. `grid`: patch rows and columns of an image are even.
All inputs are finite; a program needn't handle non-finite values.
Results may differ from the reference program's by a relative error of at most 0.02.
Values may be sent and summed in bfloat16 or wider, within the bound.
A program may use at most 64 MiB of HBM per device.

```python
import math
import jax
import jax.numpy as jnp
from jax import lax

D = 1280
HEADS = 16
HEAD = 80
PATCH_SIDE = 16
SLOTS = 256
MERGED = 64
IMAGES = 64
SEQ = 10240


def layout_helper(key):
    base = jax.random.fold_in(key, 17)
    key_rows = jax.random.fold_in(base, 1)
    key_cols = jax.random.fold_in(base, 2)
    side_half = PATCH_SIDE // 2
    heights = 2 * jax.random.randint(key_rows, (IMAGES,), 1, side_half + 1)
    widths = 2 * jax.random.randint(key_cols, (IMAGES,), 1, side_half + 1)
    return (heights.astype(jnp.int32), widths.astype(jnp.int32))


def draw_grid(key, part):
    heights, widths = layout_helper(key)
    return jnp.stack([heights, widths], axis=1).astype(jnp.int32)


def draw_prompt_pos(key, part):
    heights, widths = layout_helper(key)
    half_side = PATCH_SIDE // 2
    rows_merged = heights // 2
    cols_merged = widths // 2
    counts = (rows_merged * cols_merged).astype(jnp.int32)
    order_key = jax.random.fold_in(key, 29)
    gap_key = jax.random.fold_in(key, 31)
    order = jax.random.permutation(order_key, IMAGES).astype(jnp.int32)
    rank = jnp.argsort(order, stable=True).astype(jnp.int32)
    free_rows = (SEQ - jnp.sum(counts)).astype(jnp.int32)
    gaps = jax.random.randint(gap_key, (IMAGES,), 1, 8).astype(jnp.int32)
    cumulative = jnp.cumsum(gaps).astype(jnp.int32)
    bounds = (free_rows * cumulative // cumulative[IMAGES - 1]).astype(jnp.int32)
    earlier = jnp.sum(jnp.where(rank[None, :] < rank[:, None], counts[None, :], 0), axis=1).astype(jnp.int32)
    start = bounds[rank] + earlier
    slot = jnp.arange(half_side * half_side, dtype=jnp.int32)
    row_index = slot // half_side
    col_index = slot % half_side
    live = (row_index[None, :] < rows_merged[:, None]) & (col_index[None, :] < cols_merged[:, None])
    placed = start[:, None] + row_index[None, :] * cols_merged[:, None] + col_index[None, :]
    return jnp.where(live, placed, -1).astype(jnp.int32)


def drawn_normal(key, tag, shape):
    return jnp.clip(jax.random.normal(jax.random.fold_in(key, tag), shape, jnp.float32), -6.0, 6.0)


def draw_patches(key, part):
    values = drawn_normal(key, 41, (IMAGES, SLOTS, D))
    return values.astype(jnp.bfloat16)


def draw_vit_qkv(key, part):
    values = drawn_normal(key, 71, (D, HEADS, 3, HEAD)) * D ** (-0.5)
    return values.reshape(D, 3 * D).astype(jnp.bfloat16)


def draw_text_embeds(key, part):
    values = drawn_normal(key, 53, (SEQ, D))
    return values.astype(jnp.bfloat16)


def draw_dec_qkv(key, part):
    values = drawn_normal(key, 79, (D, HEADS, 3, HEAD)) * D ** (-0.5)
    return values.reshape(D, 3 * D).astype(jnp.bfloat16)


def steps_of(key, extent, shards, low, largest):
    level, own = 1.0, jax.random.fold_in(key, 6)
    for position, shards_of in shards:
        steps = jnp.exp(jax.random.uniform(jax.random.fold_in(own, position), (shards_of,), jnp.float32, low / len(shards), largest / len(shards)))
        level = level * jnp.repeat(steps, extent[position] // shards_of).reshape([-1 if axis == position else 1 for axis in range(len(extent))])
    return level


def gaussian(rng, extent, scale, bound, shards=(), held_as=jnp.bfloat16):
    entries = jax.random.normal(rng, extent, jnp.float32) * scale
    if len(shards) > 0:
        entries = steps_of(rng, extent, shards, -0.22, 0.18) * entries
    return jnp.clip(entries, min=-bound, max=bound).astype(held_as)


def setup_inputs(seed: int = 0) -> dict:
    key_of = jax.random.split(jax.random.key(seed), 12)
    patches = draw_patches(jax.random.fold_in(key_of[11], 71), 0)
    grid = draw_grid(jax.random.fold_in(key_of[11], 71), 0)
    vit_gain = jnp.clip(1.0 + 0.15 * jax.random.normal(key_of[2], (D,), jnp.float32), 0.25, 1.75)
    vit_qkv = draw_vit_qkv(jax.random.fold_in(key_of[11], 71), 0)
    vit_out = gaussian(key_of[4], (D, D), (D // 16) ** -0.5, 0.625, ((0, 8), (1, 64)))
    merge_weight = gaussian(key_of[5], (4, D, D), (4 * D) ** -0.5, 0.078125, ((1, 8), (2, 64)))
    text_embeds = draw_text_embeds(jax.random.fold_in(key_of[11], 71), 0)
    prompt_pos = draw_prompt_pos(jax.random.fold_in(key_of[11], 71), 0)
    dec_gain = jnp.clip(1.0 + 0.15 * jax.random.normal(key_of[8], (D,), jnp.float32), 0.25, 1.75)
    dec_qkv = draw_dec_qkv(jax.random.fold_in(key_of[11], 71), 0)
    dec_out = gaussian(key_of[10], (D, D), (D // 64) ** -0.5, 1.25, ((0, 8), (1, 64)))
    return {"patches": patches, "grid": grid, "vit_gain": vit_gain, "vit_qkv": vit_qkv, "vit_out": vit_out, "merge_weight": merge_weight, "text_embeds": text_embeds, "prompt_pos": prompt_pos, "dec_gain": dec_gain, "dec_qkv": dec_qkv, "dec_out": dec_out}


eps_norm = 1e-06

def layer_norm(values, gain):
    center = values - lax.optimization_barrier(jnp.mean(values, axis=-1, keepdims=True))
    spread = lax.optimization_barrier(jnp.mean(center * center, axis=-1, keepdims=True))
    return center * lax.rsqrt(spread + eps_norm) * gain

def rms_norm(values, gain):
    return values * lax.rsqrt(lax.optimization_barrier(jnp.mean(values * values, axis=-1, keepdims=True)) + eps_norm) * gain

def image_attention(inputs):
    query, keys, values, keep = inputs
    scores = jnp.einsum('qhd,khd->hqk', query.astype(jnp.float32), keys.astype(jnp.float32)) * HEAD ** (-0.5)
    scores = jnp.where(keep[None, None, :], scores, -jnp.inf)
    weights = jnp.exp(scores - lax.optimization_barrier(jnp.max(scores, axis=-1, keepdims=True)))
    total = lax.optimization_barrier(jnp.sum(weights, axis=-1))
    mixed = jnp.einsum('hqk,khd->qhd', weights.astype(jnp.bfloat16).astype(jnp.float32), values.astype(jnp.float32))
    mixed = mixed / jnp.transpose(total, (1, 0))[..., None]
    return mixed.astype(jnp.bfloat16).reshape(SLOTS, D)

def reference(patches, grid, vit_gain, vit_qkv, vit_out, merge_weight, text_embeds, prompt_pos, dec_gain, dec_qkv, dec_out):
    side = PATCH_SIDE
    half_side = side // 2
    slot_ids = jnp.arange(SLOTS, dtype=jnp.int32)
    keep = ((slot_ids // side)[None, :] < grid[:, 0:1]) & ((slot_ids % side)[None, :] < grid[:, 1:2])
    normed = layer_norm(patches.astype(jnp.float32), vit_gain).astype(jnp.bfloat16)
    projected = jnp.dot(normed.reshape(IMAGES * SLOTS, D), vit_qkv, preferred_element_type=jnp.float32)
    projected = projected.astype(jnp.bfloat16).reshape(IMAGES, SLOTS, HEADS, 3, HEAD)
    attended = lax.map(image_attention, (projected[:, :, :, 0], projected[:, :, :, 1], projected[:, :, :, 2], keep))
    branch = jnp.dot(attended.reshape(IMAGES * SLOTS, D), vit_out, preferred_element_type=jnp.float32)
    after = (patches.reshape(IMAGES * SLOTS, D).astype(jnp.float32) + branch).astype(jnp.bfloat16)
    grouped = after.reshape(IMAGES, half_side, 2, half_side, 2, D).transpose(0, 1, 3, 2, 4, 5)
    grouped = grouped.reshape(IMAGES * MERGED, 4 * D)
    merged = jnp.dot(grouped, merge_weight.reshape(4 * D, D), preferred_element_type=jnp.float32).astype(jnp.bfloat16)
    flat_pos = prompt_pos.reshape(-1)
    target = jnp.where(flat_pos < 0, SEQ, flat_pos).astype(jnp.int32)
    dec_in = text_embeds.at[target].set(merged, mode='drop')
    dec_normed = rms_norm(dec_in.astype(jnp.float32), dec_gain).astype(jnp.bfloat16)
    dec_proj = jnp.dot(dec_normed, dec_qkv, preferred_element_type=jnp.float32)
    dec_proj = dec_proj.astype(jnp.bfloat16).reshape(SEQ, HEADS, 3, HEAD)
    queries = dec_proj[:, :, 0].astype(jnp.float32)
    keys = dec_proj[:, :, 1].astype(jnp.float32)
    values = dec_proj[:, :, 2].astype(jnp.float32)
    block = math.gcd(SEQ, 512)
    key_pos = jnp.arange(SEQ, dtype=jnp.int32)

    def one_block(index):
        begin = (index * block).astype(jnp.int32)
        query = lax.dynamic_slice_in_dim(queries, begin, block)
        query_pos = begin + jnp.arange(block, dtype=jnp.int32)
        scores = jnp.einsum('qhd,khd->hqk', query, keys) * HEAD ** (-0.5)
        scores = jnp.where(key_pos[None, None, :] <= query_pos[None, :, None], scores, -jnp.inf)
        weights = jnp.exp(scores - lax.optimization_barrier(jnp.max(scores, axis=-1, keepdims=True)))
        total = lax.optimization_barrier(jnp.sum(weights, axis=-1))
        mixed = jnp.einsum('hqk,khd->qhd', weights.astype(jnp.bfloat16).astype(jnp.float32), values)
        mixed = mixed / jnp.transpose(total, (1, 0))[..., None]
        return mixed.astype(jnp.bfloat16).reshape(block, D)
    dec_att = lax.map(one_block, jnp.arange(SEQ // block, dtype=jnp.int32)).reshape(SEQ, D)
    dec_branch = jnp.dot(dec_att, dec_out, preferred_element_type=jnp.float32)
    return (dec_in.astype(jnp.float32) + dec_branch).astype(jnp.bfloat16)
```

```python
import functools

import jax
import jax.numpy as jnp
from jax import lax
from jax.experimental import pallas as pl
from jax.experimental.pallas import tpu as pltpu
from jax.sharding import PartitionSpec as P

HEAD = 80
SCALE = HEAD ** -0.5
EPS = 1e-6
NZ, NY, NX = 8, 8, 4
FEAT = 160
HALF = 80
ROWS = 320
BF = jnp.bfloat16
F32 = jnp.float32
MESH = pl.DeviceIdType.MESH
ORDER7 = (4, 3, 5, 2, 6, 1, 7)
ORDER3 = (2, 1, 3)


def dg(a, b, ca, cb):
    return lax.dot_general(a, b, (((ca,), (cb,)), ((), ())), preferred_element_type=F32)


def iota(shape, axis):
    return lax.broadcasted_iota(jnp.int32, shape, axis)


def kernel(
    grid_ref,
    patches_ref,
    vgain_ref,
    vqkv_ref,
    vout_ref,
    merge_ref,
    text_ref,
    ppos_ref,
    dgain_ref,
    dqkv_ref,
    dout_ref,
    out_ref,
    wbuf,
    wa,
    wm,
    wc,
    gains,
    xz,
    pz,
    rz,
    att,
    imgs,
    p3,
    r3,
    mt,
    hot,
    seen,
    txt,
    route_s,
    route_r,
    dz,
    kv,
    kt,
    qb,
    sc,
    ob,
    orx,
    attd,
    p9,
    r9,
    fin,
    zs,
    zr,
    wys,
    wyr,
    wxs,
    wxr,
    wbs,
    wbr,
    y4s,
    y4r,
    x5s,
    x5r,
    b6s,
    b6r,
    q7s,
    q7r,
    k7s,
    k7r,
    o8s,
    o8r,
    sbs,
    sbr,
):
    w = lax.axis_index("wide")
    z = lax.axis_index("narrow")
    y, x, c = w // 8, (w // 2) % 4, w % 2

    def dev(yy, xx, cc, zz):
        return (yy * 8 + xx * 2 + cc, zz)

    def zpeer(k):
        return dev(y, x, c, (z + k) % NZ)

    def ypeer(k):
        return dev((y + k) % NY, x, c, z)

    def xpeer(k):
        return dev(y, (x + k) % NX, c, z)

    sib = dev(y, x, 1 - c, z)

    def rcopy(src, dst, s, r, to):
        return pltpu.make_async_remote_copy(
            src_ref=src, dst_ref=dst, send_sem=s, recv_sem=r, device_id=to, device_id_type=MESH
        )

    barrier = pltpu.get_barrier_semaphore()
    peers = [zpeer(k) for k in range(1, 8)] + [ypeer(k) for k in range(1, 8)]
    peers += [xpeer(k) for k in range(1, 4)] + [sib]
    for p in peers:
        pl.semaphore_signal(barrier, inc=1, device_id=p, device_id_type=MESH)

    pending = []

    slot_to = iota((256, 256), 1)
    sub, tok = slot_to // 64, slot_to % 64
    want = (2 * (tok // 8) + sub // 2) * 16 + 2 * (tok % 8) + sub % 2
    perm = (iota((256, 256), 0) == want).astype(F32).astype(BF)
    xz[z] = dg(patches_ref[0], perm, 0, 0).astype(BF)

    wbuf[0, c, x, y] = jnp.concatenate([vqkv_ref[...], vout_ref[...].T], axis=1)
    wbuf[1, c, x, y] = merge_ref[...].reshape(4 * FEAT, 20).T
    wbuf[2, c, x, y] = jnp.concatenate([dqkv_ref[...], dout_ref[...].T], axis=1)
    place = (iota((FEAT, ROWS), 1) == iota((FEAT, ROWS), 0) + FEAT * c).astype(F32).astype(BF)
    own_text = dg(text_ref[...], place, 0, 0).astype(BF)
    txt[0, 0] = own_text[:HALF]
    txt[0, 1] = own_text[HALF:]

    pl.semaphore_wait(barrier, len(peers))

    def z_gather(phase, buf):
        cps = {k: rcopy(buf, buf, zs.at[phase, k], zr.at[phase, k], zpeer(k)) for k in ORDER7}
        for k in ORDER7:
            cps[k].start()
        return cps

    p1 = z_gather(0, xz.at[z])

    def wy(g, k):
        ref = wbuf.at[g, c, x, y]
        return rcopy(ref, ref, wys.at[g, k], wyr.at[g, k], ypeer(k))

    def wx(g, k):
        ref = wbuf.at[g, c, x]
        return rcopy(ref, ref, wxs.at[g, k], wxr.at[g, k], xpeer(k))

    def wb(g, k):
        ref = wbuf.at[g, c, (x + NX - k) % NX]
        return rcopy(ref, ref, wbs.at[g, k], wbr.at[g, k], sib)

    for g in range(3):
        for k in ORDER7:
            wy(g, k).start()
    text_cp = rcopy(txt.at[0, 1 - c], txt.at[1, 0], sbs.at[0], sbr.at[0], sib)
    text_cp.start()

    def y_done(g):
        for k in ORDER7:
            wy(g, k).wait_recv()

    def x_go(g):
        for k in ORDER3:
            wx(g, k).start()
        wb(g, 0).start()

    def x_done(g):
        for k in ORDER3:
            wx(g, k).wait_recv()
            wb(g, k).start()

    def b_done(g):
        for k in range(4):
            wb(g, k).wait_recv()

    def w_sent(g):
        for k in ORDER7:
            wy(g, k).wait_send()
        for k in ORDER3:
            wx(g, k).wait_send()
        for k in range(4):
            wb(g, k).wait_send()

    for k in range(10):
        at = slice(128 * k, 128 * k + 128)
        gains[0, at, :] = jnp.broadcast_to(vgain_ref[:, at], (128, 128)).T
        gains[1, at, :] = jnp.broadcast_to(dgain_ref[:, at], (128, 128)).T

    y_done(0)
    x_go(0)

    def table(t, carry):
        base = ROWS * (4 * y + t)
        rows = iota((ROWS, 128), 0) + base
        for j in range(NY):
            tokens = ppos_ref[pl.ds(4 * j + x, 1), :]
            hot[t, :, 128 * j : 128 * j + 128] = (rows == tokens).astype(F32).astype(BF)
        return carry

    lax.fori_loop(0, NX, table, 0)

    mine = iota((ROWS, 128), 0) + ROWS * (4 * y + x)

    def mark(j, carry):
        return jnp.maximum(carry, (mine == ppos_ref[pl.ds(j, 1), :]).astype(F32))

    hits = lax.fori_loop(0, 32, mark, jnp.zeros((ROWS, 128), F32)).astype(BF)
    seen[...] = dg(jnp.ones((16, 128), BF), hits, 1, 1)

    x_done(0)
    y_done(1)
    x_go(1)
    b_done(0)

    def pieces(g, row):
        return [wbuf[g, cc, xx, row] for xx in range(NX) for cc in range(2)]

    def build_a(row, carry):
        wa[pl.ds(pl.multiple_of(FEAT * row, 16), FEAT), :] = jnp.concatenate(pieces(0, row), axis=0)
        return carry

    lax.fori_loop(0, NY, build_a, 0)

    for k in ORDER7:
        p1[k].wait_recv()
    xa = xz[...].reshape(8 * FEAT, 256).astype(F32)
    mean = jnp.sum(xa, axis=0, keepdims=True) * (1.0 / 1280.0)
    xa = xa - mean
    var = jnp.sum(xa * xa, axis=0, keepdims=True) * (1.0 / 1280.0)
    gain = jnp.concatenate([gains[0], gains[0]], axis=1)
    normed = (xa * lax.rsqrt(var + EPS) * gain).astype(BF)
    proj = dg(wa[:, :512], normed, 0, 0).astype(BF)
    slot = iota((256, 256), 0)
    sub, tok = slot // 64, slot % 64
    row_id = 2 * (tok // 8) + sub // 2
    col_id = 2 * (tok % 8) + sub % 2
    keep = (row_id < grid_ref[0, 0]) & (col_id < grid_ref[0, 1])
    att[0:96] = jnp.zeros((96, 256), BF)
    for h in range(2):
        qh = proj[240 * h : 240 * h + 80]
        kh = proj[240 * h + 80 : 240 * h + 160]
        vh = proj[240 * h + 160 : 240 * h + 240]
        s = dg(kh, qh, 0, 0) * SCALE
        s = jnp.where(keep, s, -jnp.inf)
        p = jnp.exp(s - jnp.max(s, axis=0, keepdims=True))
        total = jnp.sum(p, axis=0, keepdims=True)
        o = dg(vh, p.astype(BF), 1, 0) / total
        att[96 + 80 * h : 176 + 80 * h] = o.astype(BF)
    pz[...] = dg(wa[:, 384:640], att[...], 1, 0).astype(BF).reshape(8, FEAT, 256)

    def z_scatter(phase, src, dst):
        cps = {
            k: rcopy(src.at[(z + k) % NZ], dst.at[z], zs.at[phase, k], zr.at[phase, k], zpeer(k))
            for k in ORDER7
        }
        for k in ORDER7:
            cps[k].start()
        dst[z] = src[z]
        return cps

    p2 = z_scatter(1, pz, rz)

    x_done(1)
    y_done(2)
    x_go(2)
    b_done(1)

    def build_m(row, carry):
        parts = [wbuf[1, cc, 2 * c + xx, row] for xx in range(2) for cc in range(2)]
        wm[pl.ds(pl.multiple_of(HALF * row, 16), HALF), :] = jnp.concatenate(parts, axis=0)
        return carry

    lax.fori_loop(0, NY, build_m, 0)

    def sum8(ref):
        total = ref[0].astype(F32)
        for j in range(1, 8):
            total = total + ref[j].astype(F32)
        return total

    for k in ORDER7:
        p2[k].wait_recv()
    after = (xz[z].astype(F32) + sum8(rz)).astype(BF)
    imgs[c] = after
    e1 = rcopy(imgs.at[c], imgs.at[c], sbs.at[1], sbr.at[1], sib)
    e1.start()
    e1.wait_recv()
    first, second = imgs[0], imgs[1]
    left = iota((FEAT, 128), 1) < 64
    stack = []
    for t in range(2):
        a, b = first[:, 128 * t : 128 * t + 128], second[:, 128 * t : 128 * t + 128]
        stack.append(jnp.where(left, a, pltpu.roll(b, 64, 1)))
        stack.append(jnp.where(left, pltpu.roll(a, 64, 1), b))
    grouped = jnp.concatenate(stack, axis=0)
    p3[...] = dg(wm[...], grouped, 1, 0).astype(BF).reshape(8, HALF, 128)
    c3 = z_scatter(2, p3, r3)

    x_done(2)
    b_done(2)

    def build_c(row, carry):
        wc[pl.ds(pl.multiple_of(FEAT * row, 16), FEAT), :] = jnp.concatenate(pieces(2, row), axis=0)
        return carry

    lax.fori_loop(0, NY, build_c, 0)

    for k in ORDER7:
        c3[k].wait_recv()
    mt[y] = sum8(r3).astype(BF)
    c4 = {k: rcopy(mt.at[y], mt.at[y], y4s.at[k], y4r.at[k], ypeer(k)) for k in ORDER7}
    for k in ORDER7:
        c4[k].start()
    for k in ORDER7:
        c4[k].wait_recv()
    tokens = jnp.concatenate([mt[j] for j in range(8)], axis=1)

    def routed(t):
        return dg(tokens, hot[t], 1, 1).astype(BF)

    c5 = {}
    for k in ORDER3:
        to = (x + k) % NX
        route_s[k] = routed(to)
        c5[k] = rcopy(route_s.at[k], route_r.at[k], x5s.at[k], x5r.at[k], xpeer(k))
        c5[k].start()
    image = routed(x).astype(F32)
    text_cp.wait_recv()
    my_text = txt[0, c].astype(F32) + txt[1, 0].astype(F32)
    for k in ORDER3:
        c5[k].wait_recv()
        image = image + route_r[k].astype(F32)
    dec_in = jnp.where(seen[0:1, :] > 0.5, image, my_text)
    dz[z, c] = dec_in.astype(BF)

    p6 = z_gather(3, dz.at[z, c])

    def b6(k):
        ref = dz.at[(z + NZ - k) % NZ, c]
        return rcopy(ref, ref, b6s.at[k], b6r.at[k], sib)

    b6(0).start()
    for k in ORDER7:
        p6[k].wait_recv()
        b6(k).start()
    for k in (0,) + ORDER7:
        b6(k).wait_recv()
    xd = dz[...].reshape(1280, ROWS).astype(F32)
    power = jnp.sum(xd * xd, axis=0, keepdims=True) * (1.0 / 1280.0)
    g1 = gains[1]
    gain = jnp.concatenate([g1, g1, g1[:, :64]], axis=1)
    normed = (xd * lax.rsqrt(power + EPS) * gain).astype(BF)
    proj = dg(wc[:, :512], normed, 0, 0).astype(BF)
    proj = jnp.where(c == 0, proj[:240], proj[240:480])
    qb[y] = proj[:80]
    kv[x] = proj[80:240]

    def q_copy(k):
        ref = qb.at[y]
        return rcopy(ref, ref, q7s.at[k], q7r.at[k], dev((y + NY - k) % NY, x, c, z))

    c7 = {k: rcopy(kv.at[x], kv.at[x], k7s.at[k], k7r.at[k], xpeer(k)) for k in ORDER3}
    for k in ORDER3:
        c7[k].start()
    for k in range(1, 8):

        @pl.when(y >= k)
        def _():
            q_copy(k).start()

    for k in ORDER3:
        c7[k].wait_recv()
    for t in range(NX):
        kt[t] = kv[t, :80].astype(F32).T.astype(BF)

    def o_copy(k):
        return rcopy(ob.at[k], orx.at[y], o8s.at[k], o8r.at[k], dev((y + k) % NY, x, c, z))

    def q_block(k, carry):
        @pl.when(k > 0)
        def _():
            q_copy(k).wait_recv()

        q = qb[y + k]
        limit = 1280 * k + ROWS * x + iota((ROWS, ROWS), 1)
        best = jnp.full((1, ROWS), -jnp.inf, F32)
        for t in range(NX):
            s = dg(kt[t], q, 1, 0) * SCALE
            s = jnp.where(iota((ROWS, ROWS), 0) + ROWS * t <= limit, s, -jnp.inf)
            best = jnp.maximum(best, jnp.max(s, axis=0, keepdims=True))
            sc[t] = s
        total = jnp.zeros((1, ROWS), F32)
        o = jnp.zeros((80, ROWS), F32)
        for t in range(NX):
            p = jnp.exp(sc[t] - best)
            total = total + jnp.sum(p, axis=0, keepdims=True)
            o = o + dg(kv[t, 80:], p.astype(BF), 1, 0)
        ob[k, :80] = (o / total).astype(BF)
        lse = best + jnp.log(total)
        hi = lse.astype(BF).astype(F32)
        mid = (lse - hi).astype(BF).astype(F32)
        low = lse - hi - mid
        at = iota((16, ROWS), 0)
        rows = jnp.where(at == 0, hi, jnp.where(at == 1, mid, jnp.where(at == 2, low, 0.0)))
        ob[k, 80:] = rows.astype(BF)

        @pl.when(k > 0)
        def _():
            o_copy(k).start()

        return carry

    lax.fori_loop(0, NY - y, q_block, 0)
    orx[y] = ob[0]
    for k in range(1, 8):

        @pl.when(y >= k)
        def _():
            rcopy(ob.at[k], orx.at[y - k], o8s.at[k], o8r.at[k], ypeer(0 - k)).wait_recv()

    def lse_of(j):
        return jnp.sum(orx[j, 80:].astype(F32), axis=0, keepdims=True)

    peak = lax.fori_loop(0, y + 1, lambda j, m: jnp.maximum(m, lse_of(j)), jnp.full((1, ROWS), -jnp.inf, F32))

    def merge_part(j, carry):
        o, total = carry
        share = jnp.exp(lse_of(j) - peak)
        return o + orx[j, :80].astype(F32) * share, total + share

    o, total = lax.fori_loop(
        0, y + 1, merge_part, (jnp.zeros((80, ROWS), F32), jnp.zeros((1, ROWS), F32))
    )
    attd[c] = (o / total).astype(BF)
    e2 = rcopy(attd.at[c], attd.at[c], sbs.at[2], sbr.at[2], sib)
    e2.start()
    e2.wait_recv()
    both = jnp.concatenate([jnp.zeros((96, ROWS), BF), attd[0], attd[1]], axis=0)
    for j in range(8):
        rows = wc[pl.ds(pl.multiple_of(FEAT * j + HALF * c, 16), HALF), 384:640]
        p9[j] = dg(rows, both, 1, 0).astype(BF)
    c9 = z_scatter(4, p9, r9)
    for k in ORDER7:
        c9[k].wait_recv()
    fin[c] = (dz[z, c].astype(F32) + sum8(r9)).astype(BF)
    e3 = rcopy(fin.at[c], fin.at[c], sbs.at[3], sbr.at[3], sib)
    e3.start()
    e3.wait_recv()
    out_ref[...] = dg(place, jnp.concatenate([fin[0], fin[1]], axis=0), 1, 1).astype(BF)

    for cps in (p1, p2, c3, c4, p6, c9):
        for k in ORDER7:
            cps[k].wait_send()
    for cps in (c5, c7):
        for k in ORDER3:
            cps[k].wait_send()
    for g in range(3):
        w_sent(g)
    for k in range(8):
        b6(k).wait_send()
    for k in range(1, 8):

        @pl.when(y >= k)
        def _():
            q_copy(k).wait_send()

        @pl.when(y + k < NY)
        def _():
            o_copy(k).wait_send()

    for cp in (text_cp, e1, e2, e3):
        cp.wait_send()


def shards(
    patches,
    grid,
    vit_gain,
    vit_qkv,
    vit_out,
    merge_weight,
    text_embeds,
    prompt_pos,
    dec_gain,
    dec_qkv,
    dec_out,
):
    vm = pl.BlockSpec(memory_space=pltpu.VMEM)
    dma = pltpu.SemaphoreType.DMA
    scratch = [
        pltpu.VMEM((3, 2, NX, NY, 20, 640), BF),
        pltpu.VMEM((1280, 640), BF),
        pltpu.VMEM((640, 640), BF),
        pltpu.VMEM((1280, 640), BF),
        pltpu.VMEM((2, 1280, 128), F32),
        pltpu.VMEM((8, FEAT, 256), BF),
        pltpu.VMEM((8, FEAT, 256), BF),
        pltpu.VMEM((8, FEAT, 256), BF),
        pltpu.VMEM((256, 256), BF),
        pltpu.VMEM((2, FEAT, 256), BF),
        pltpu.VMEM((8, HALF, 128), BF),
        pltpu.VMEM((8, HALF, 128), BF),
        pltpu.VMEM((8, HALF, 128), BF),
        pltpu.VMEM((NX, ROWS, 1024), BF),
        pltpu.VMEM((16, ROWS), F32),
        pltpu.VMEM((2, 2, HALF, ROWS), BF),
        pltpu.VMEM((NX, HALF, ROWS), BF),
        pltpu.VMEM((NX, HALF, ROWS), BF),
        pltpu.VMEM((8, 2, HALF, ROWS), BF),
        pltpu.VMEM((NX, 160, ROWS), BF),
        pltpu.VMEM((NX, ROWS, 80), BF),
        pltpu.VMEM((8, 80, ROWS), BF),
        pltpu.VMEM((NX, ROWS, ROWS), F32),
        pltpu.VMEM((8, 96, ROWS), BF),
        pltpu.VMEM((8, 96, ROWS), BF),
        pltpu.VMEM((2, 80, ROWS), BF),
        pltpu.VMEM((8, HALF, ROWS), BF),
        pltpu.VMEM((8, HALF, ROWS), BF),
        pltpu.VMEM((2, HALF, ROWS), BF),
    ]
    sems = []
    for shape in ((5, 8), (3, 8), (3, 4), (3, 4), (8,), (4,), (8,), (8,), (4,), (8,), (4,)):
        sems += [dma(shape), dma(shape)]
    return pl.pallas_call(
        kernel,
        out_shape=jax.ShapeDtypeStruct((160, 160), BF),
        in_specs=[pl.BlockSpec(memory_space=pltpu.SMEM)] + [vm] * 10,
        out_specs=vm,
        scratch_shapes=scratch + sems,
        compiler_params=pltpu.CompilerParams(
            collective_id=0, has_side_effects=True, vmem_limit_bytes=60 << 20
        ),
        name="layer",
    )(
        grid,
        patches,
        vit_gain.reshape(1, 1280),
        vit_qkv,
        vit_out,
        merge_weight,
        text_embeds,
        prompt_pos.reshape(32, 128),
        dec_gain.reshape(1, 1280),
        dec_qkv,
        dec_out,
    )


def solution(mesh):
    placed = (
        P("wide", None, "narrow"),
        P("wide", None),
        P(),
        P("wide", "narrow"),
        P("narrow", "wide"),
        P(None, "narrow", "wide"),
        P("wide", "narrow"),
        P(),
        P(),
        P("wide", "narrow"),
        P("narrow", "wide"),
    )
    return jax.shard_map(
        shards, mesh=mesh, in_specs=placed, out_specs=P("wide", "narrow"), check_vma=False
    )
```

```python
import functools

import jax
import jax.numpy as jnp
from jax import lax
from jax.experimental import pallas as pl
from jax.experimental.pallas import tpu as pltpu
from jax.sharding import PartitionSpec as P

HEAD = 80
SCALE = HEAD ** -0.5
EPS = 1e-6
NZ, NY, NX = 8, 8, 4
FEAT = 160
HALF = 80
ROWS = 320
BF = jnp.bfloat16
F32 = jnp.float32
MESH = pl.DeviceIdType.MESH
ORDER7 = (4, 3, 5, 2, 6, 1, 7)
NEAR7 = (1, 7, 2, 6, 3, 5, 4)
ORDER3 = (2, 1, 3)


def dg(a, b, ca, cb):
    return lax.dot_general(a, b, (((ca,), (cb,)), ((), ())), preferred_element_type=F32)


def iota(shape, axis):
    return lax.broadcasted_iota(jnp.int32, shape, axis)


def kernel(
    grid_ref,
    patches_ref,
    vgain_ref,
    vqkv_ref,
    vout_ref,
    merge_ref,
    text_ref,
    ppos_ref,
    dgain_ref,
    dqkv_ref,
    dout_ref,
    out_ref,
    wbuf,
    wa,
    wm,
    wc,
    gains,
    xz,
    pz,
    rz,
    att,
    imgs,
    p3,
    r3,
    mt,
    hot,
    seen,
    txt,
    route_s,
    route_r,
    dz,
    kv,
    kt,
    qb,
    sc,
    ob,
    orx,
    attd,
    p9,
    r9,
    fin,
    zs,
    zr,
    wys,
    wyr,
    wxs,
    wxr,
    wbs,
    wbr,
    y4s,
    y4r,
    x5s,
    x5r,
    b6s,
    b6r,
    q7s,
    q7r,
    k7s,
    k7r,
    o8s,
    o8r,
    sbs,
    sbr,
):
    w = lax.axis_index("wide")
    z = lax.axis_index("narrow")
    y, x, c = w // 8, (w // 2) % 4, w % 2

    def dev(yy, xx, cc, zz):
        return (yy * 8 + xx * 2 + cc, zz)

    def zpeer(k):
        return dev(y, x, c, (z + k) % NZ)

    def ypeer(k):
        return dev((y + k) % NY, x, c, z)

    def xpeer(k):
        return dev(y, (x + k) % NX, c, z)

    sib = dev(y, x, 1 - c, z)

    def rcopy(src, dst, s, r, to):
        return pltpu.make_async_remote_copy(
            src_ref=src, dst_ref=dst, send_sem=s, recv_sem=r, device_id=to, device_id_type=MESH
        )

    barrier = pltpu.get_barrier_semaphore()
    peers = [zpeer(k) for k in range(1, 8)] + [ypeer(k) for k in range(1, 8)]
    peers += [xpeer(k) for k in range(1, 4)] + [sib]
    for p in peers:
        pl.semaphore_signal(barrier, inc=1, device_id=p, device_id_type=MESH)

    slot_to = iota((256, 256), 1)
    sub, tok = slot_to // 64, slot_to % 64
    want = (2 * (tok // 8) + sub // 2) * 16 + 2 * (tok % 8) + sub % 2
    perm = (iota((256, 256), 0) == want).astype(F32).astype(BF)
    xz[z] = dg(patches_ref[...], perm, 1, 0).astype(BF)

    wbuf[0, c, x, y] = jnp.concatenate([vqkv_ref[...], vout_ref[...]], axis=1)
    wbuf[1, c, x, y] = jnp.concatenate([merge_ref[:, j, :] for j in range(4)], axis=1)
    wbuf[2, c, x, y] = jnp.concatenate([dqkv_ref[...], dout_ref[...]], axis=1)
    place = (iota((FEAT, ROWS), 1) == iota((FEAT, ROWS), 0) + FEAT * c).astype(F32).astype(BF)
    own_text = dg(text_ref[...], place, 0, 0).astype(BF)
    txt[0, 0] = own_text[:HALF]
    txt[0, 1] = own_text[HALF:]

    pl.semaphore_wait(barrier, len(peers))

    def z_gather(phase, buf):
        cps = {k: rcopy(buf, buf, zs.at[phase, k], zr.at[phase, k], zpeer(k)) for k in ORDER7}
        for k in ORDER7:
            cps[k].start()
        return cps

    p1 = z_gather(0, xz.at[z])

    def wy(g, k):
        ref = wbuf.at[g, c, x, y]
        return rcopy(ref, ref, wys.at[g, k], wyr.at[g, k], ypeer(k))

    def wx(g, k):
        ref = wbuf.at[g, c, x]
        return rcopy(ref, ref, wxs.at[g, k], wxr.at[g, k], xpeer(k))

    def wb(g, k):
        ref = wbuf.at[g, c, (x + NX - k) % NX]
        return rcopy(ref, ref, wbs.at[g, k], wbr.at[g, k], sib)

    def wx_piece(g, k, j):
        ref = wbuf.at[g, c, x, (y + NY - k) % NY]
        return rcopy(ref, ref, wxs.at[g, j], wxr.at[g, j], xpeer(j))

    def y_go(g):
        for k in NEAR7:
            wy(g, k).start()
        for j in ORDER3:
            wx_piece(g, 0, j).start()

    y_go(0)
    text_cp = rcopy(txt.at[0, 1 - c], txt.at[1, 0], sbs.at[0], sbr.at[0], sib)
    text_cp.start()

    def y_done(g):
        for k in NEAR7:
            wy(g, k).wait_recv()
            for j in ORDER3:
                wx_piece(g, k, j).start()
        wb(g, 0).start()

    def x_done(g):
        for k in ORDER3:
            wx(g, k).wait_recv()
            wb(g, k).start()

    def b_done(g):
        for k in range(4):
            wb(g, k).wait_recv()

    def w_sent(g):
        for k in ORDER7:
            wy(g, k).wait_send()
        for k in ORDER3:
            wx(g, k).wait_send()
        for k in range(4):
            wb(g, k).wait_send()

    for k in range(10):
        at = slice(128 * k, 128 * k + 128)
        gains[0, at, :] = jnp.broadcast_to(vgain_ref[k : k + 1, :], (128, 128)).T
        gains[1, at, :] = jnp.broadcast_to(dgain_ref[k : k + 1, :], (128, 128)).T

    y_done(0)
    y_go(1)

    def chip_tokens(j):
        return jnp.concatenate([ppos_ref[pl.ds(2 * j, 1), :], ppos_ref[pl.ds(2 * j + 1, 1), :]], axis=1)

    def table(t, carry):
        base = ROWS * (4 * y + t)
        rows = iota((ROWS, 128), 0) + base
        for j in range(NY):
            tokens = chip_tokens(4 * j + x)
            hot[t, :, 128 * j : 128 * j + 128] = (rows == tokens).astype(F32).astype(BF)
        return carry

    lax.fori_loop(0, NX, table, 0)

    mine = iota((ROWS, 128), 0) + ROWS * (4 * y + x)

    def mark(j, carry):
        return jnp.maximum(carry, (mine == chip_tokens(j)).astype(F32))

    hits = lax.fori_loop(0, 32, mark, jnp.zeros((ROWS, 128), F32)).astype(BF)
    seen[...] = dg(jnp.ones((16, 128), BF), hits, 1, 1)

    x_done(0)
    y_done(1)
    y_go(2)
    b_done(0)

    def pieces(g, row):
        return [wbuf[g, cc, xx, row] for xx in range(NX) for cc in range(2)]

    def build_a(row, carry):
        wa[pl.ds(pl.multiple_of(FEAT * row, 16), FEAT), :] = jnp.concatenate(pieces(0, row), axis=0)
        return carry

    lax.fori_loop(0, NY, build_a, 0)

    for k in ORDER7:
        p1[k].wait_recv()
    xa = xz[...].reshape(8 * FEAT, 256).astype(F32)
    mean = jnp.sum(xa, axis=0, keepdims=True) * (1.0 / 1280.0)
    xa = xa - mean
    var = jnp.sum(xa * xa, axis=0, keepdims=True) * (1.0 / 1280.0)
    gain = jnp.concatenate([gains[0], gains[0]], axis=1)
    normed = (xa * lax.rsqrt(var + EPS) * gain).astype(BF)
    proj = dg(wa[:, :512], normed, 0, 0).astype(BF)
    slot = iota((256, 256), 0)
    sub, tok = slot // 64, slot % 64
    row_id = 2 * (tok // 8) + sub // 2
    col_id = 2 * (tok % 8) + sub % 2
    keep = (row_id < grid_ref[0, 0]) & (col_id < grid_ref[0, 1])
    att[0:96] = jnp.zeros((96, 256), BF)
    for h in range(2):
        qh = proj[240 * h : 240 * h + 80]
        kh = proj[240 * h + 80 : 240 * h + 160]
        vh = proj[240 * h + 160 : 240 * h + 240]
        s = dg(kh, qh, 0, 0) * SCALE
        s = jnp.where(keep, s, -jnp.inf)
        p = jnp.exp(s - jnp.max(s, axis=0, keepdims=True))
        total = jnp.sum(p, axis=0, keepdims=True)
        o = dg(vh, p.astype(BF), 1, 0) / total
        att[96 + 80 * h : 176 + 80 * h] = o.astype(BF)
    pz[...] = dg(wa[:, 384:640], att[...], 1, 0).astype(BF).reshape(8, FEAT, 256)

    def z_scatter(phase, src, dst):
        cps = {
            k: rcopy(src.at[(z + k) % NZ], dst.at[z], zs.at[phase, k], zr.at[phase, k], zpeer(k))
            for k in ORDER7
        }
        for k in ORDER7:
            cps[k].start()
        dst[z] = src[z]
        return cps

    p2 = z_scatter(1, pz, rz)

    x_done(1)
    y_done(2)
    b_done(1)

    def build_m(row, carry):
        parts = [wbuf[1, cc, 2 * c + xx, row] for xx in range(2) for cc in range(2)]
        wm[pl.ds(pl.multiple_of(HALF * row, 16), HALF), :] = jnp.concatenate(parts, axis=0)
        return carry

    lax.fori_loop(0, NY, build_m, 0)

    def sum8(ref):
        total = ref[0].astype(F32)
        for j in range(1, 8):
            total = total + ref[j].astype(F32)
        return total

    for k in ORDER7:
        p2[k].wait_recv()
    after = (xz[z].astype(F32) + sum8(rz)).astype(BF)
    imgs[c] = after
    e1 = rcopy(imgs.at[c], imgs.at[c], sbs.at[1], sbr.at[1], sib)
    e1.start()
    e1.wait_recv()
    first, second = imgs[0], imgs[1]
    left = iota((FEAT, 128), 1) < 64
    stack = []
    for t in range(2):
        a, b = first[:, 128 * t : 128 * t + 128], second[:, 128 * t : 128 * t + 128]
        stack.append(jnp.where(left, a, pltpu.roll(b, 64, 1)))
        stack.append(jnp.where(left, pltpu.roll(a, 64, 1), b))
    grouped = jnp.concatenate(stack, axis=0)
    p3[...] = dg(wm[...], grouped, 1, 0).astype(BF).reshape(8, HALF, 128)
    c3 = z_scatter(2, p3, r3)

    x_done(2)
    b_done(2)

    def build_c(row, carry):
        wc[pl.ds(pl.multiple_of(FEAT * row, 16), FEAT), :] = jnp.concatenate(pieces(2, row), axis=0)
        return carry

    lax.fori_loop(0, NY, build_c, 0)

    for k in ORDER7:
        c3[k].wait_recv()
    mt[y] = sum8(r3).astype(BF)
    c4 = {k: rcopy(mt.at[y], mt.at[y], y4s.at[k], y4r.at[k], ypeer(k)) for k in ORDER7}
    for k in ORDER7:
        c4[k].start()
    for k in ORDER7:
        c4[k].wait_recv()
    tokens = jnp.concatenate([mt[j] for j in range(8)], axis=1)

    def routed(t):
        return dg(tokens, hot[t], 1, 1).astype(BF)

    c5 = {}
    for k in ORDER3:
        to = (x + k) % NX
        route_s[k] = routed(to)
        c5[k] = rcopy(route_s.at[k], route_r.at[k], x5s.at[k], x5r.at[k], xpeer(k))
        c5[k].start()
    image = routed(x).astype(F32)
    text_cp.wait_recv()
    my_text = txt[0, c].astype(F32) + txt[1, 0].astype(F32)
    for k in ORDER3:
        c5[k].wait_recv()
        image = image + route_r[k].astype(F32)
    dec_in = jnp.where(seen[0:1, :] > 0.5, image, my_text)
    dz[z, c] = dec_in.astype(BF)

    def ring(right, s):
        if right:
            at, rows = (z + NZ - s) % NZ, pl.ds(0, 48)
        else:
            at, rows = (z + s) % NZ, pl.ds(48, 32)
        ref = dz.at[at, c] if s < 3 else dz.at[at, c, rows]
        sem = s if right else 4 + s
        return rcopy(ref, ref, zs.at[3, sem], zr.at[3, sem], zpeer(1 if right else NZ - 1))

    ring(True, 0).start()
    ring(False, 0).start()

    def b6(k):
        ref = dz.at[(z + NZ - k) % NZ, c]
        return rcopy(ref, ref, b6s.at[k], b6r.at[k], sib)

    b6(0).start()
    for s in range(4):
        ring(True, s).wait_recv()
        if s < 3:
            ring(True, s + 1).start()
        ring(False, s).wait_recv()
        if s < 3:
            ring(False, s + 1).start()
            b6(s + 1).start()
            b6(7 - s).start()
        else:
            b6(4).start()
    for k in range(8):
        b6(k).wait_recv()
    xd = dz[...].reshape(1280, ROWS).astype(F32)
    power = jnp.sum(xd * xd, axis=0, keepdims=True) * (1.0 / 1280.0)
    g1 = gains[1]
    gain = jnp.concatenate([g1, g1, g1[:, :64]], axis=1)
    normed = (xd * lax.rsqrt(power + EPS) * gain).astype(BF)
    proj = dg(wc[:, :512], normed, 0, 0).astype(BF)
    proj = jnp.where(c == 0, proj[:240], proj[240:480])
    qb[y] = proj[:80]
    kv[x] = proj[80:240]

    def q_copy(k):
        ref = qb.at[y]
        return rcopy(ref, ref, q7s.at[k], q7r.at[k], dev((y + NY - k) % NY, x, c, z))

    c7 = {k: rcopy(kv.at[x], kv.at[x], k7s.at[k], k7r.at[k], xpeer(k)) for k in ORDER3}
    for k in ORDER3:
        c7[k].start()
    for k in range(1, 8):

        @pl.when(y >= k)
        def _():
            q_copy(k).start()

    for k in ORDER3:
        c7[k].wait_recv()
    for t in range(NX):
        kt[t] = kv[t, :80].astype(F32).T.astype(BF)

    def o_copy(k):
        return rcopy(ob.at[k], orx.at[y], o8s.at[k], o8r.at[k], dev((y + k) % NY, x, c, z))

    def q_block(k, carry):
        @pl.when(k > 0)
        def _():
            q_copy(k).wait_recv()

        q = qb[y + k]
        limit = 1280 * k + ROWS * x + iota((ROWS, ROWS), 1)
        best = jnp.full((1, ROWS), -jnp.inf, F32)
        for t in range(NX):
            s = dg(kt[t], q, 1, 0) * SCALE
            s = jnp.where(iota((ROWS, ROWS), 0) + ROWS * t <= limit, s, -jnp.inf)
            best = jnp.maximum(best, jnp.max(s, axis=0, keepdims=True))
            sc[t] = s
        total = jnp.zeros((1, ROWS), F32)
        o = jnp.zeros((80, ROWS), F32)
        for t in range(NX):
            p = jnp.exp(sc[t] - best)
            total = total + jnp.sum(p, axis=0, keepdims=True)
            o = o + dg(kv[t, 80:], p.astype(BF), 1, 0)
        ob[k, :80] = (o / total).astype(BF)
        lse = best + jnp.log(total)
        hi = lse.astype(BF).astype(F32)
        mid = (lse - hi).astype(BF).astype(F32)
        low = lse - hi - mid
        at = iota((16, ROWS), 0)
        rows = jnp.where(at == 0, hi, jnp.where(at == 1, mid, jnp.where(at == 2, low, 0.0)))
        ob[k, 80:] = rows.astype(BF)

        @pl.when(k > 0)
        def _():
            o_copy(k).start()

        return carry

    lax.fori_loop(0, NY - y, q_block, 0)
    orx[y] = ob[0]
    for k in range(1, 8):

        @pl.when(y >= k)
        def _():
            rcopy(ob.at[k], orx.at[y - k], o8s.at[k], o8r.at[k], ypeer(0 - k)).wait_recv()

    def lse_of(j):
        return jnp.sum(orx[j, 80:].astype(F32), axis=0, keepdims=True)

    peak = lax.fori_loop(0, y + 1, lambda j, m: jnp.maximum(m, lse_of(j)), jnp.full((1, ROWS), -jnp.inf, F32))

    def merge_part(j, carry):
        o, total = carry
        share = jnp.exp(lse_of(j) - peak)
        return o + orx[j, :80].astype(F32) * share, total + share

    o, total = lax.fori_loop(
        0, y + 1, merge_part, (jnp.zeros((80, ROWS), F32), jnp.zeros((1, ROWS), F32))
    )
    attd[c] = (o / total).astype(BF)
    e2 = rcopy(attd.at[c], attd.at[c], sbs.at[2], sbr.at[2], sib)
    e2.start()
    e2.wait_recv()
    both = jnp.concatenate([jnp.zeros((96, ROWS), BF), attd[0], attd[1]], axis=0)
    for j in range(8):
        rows = wc[pl.ds(pl.multiple_of(FEAT * j + HALF * c, 16), HALF), 384:640]
        p9[j] = dg(rows, both, 1, 0).astype(BF)
    c9 = z_scatter(4, p9, r9)
    for k in ORDER7:
        c9[k].wait_recv()
    fin[c] = (dz[z, c].astype(F32) + sum8(r9)).astype(BF)
    e3 = rcopy(fin.at[c], fin.at[c], sbs.at[3], sbr.at[3], sib)
    e3.start()
    e3.wait_recv()
    out_ref[...] = dg(place, jnp.concatenate([fin[0], fin[1]], axis=0), 1, 1).astype(BF)

    for s in range(4):
        ring(True, s).wait_send()
        ring(False, s).wait_send()
    for cps in (p1, p2, c3, c4, c9):
        for k in ORDER7:
            cps[k].wait_send()
    for cps in (c5, c7):
        for k in ORDER3:
            cps[k].wait_send()
    for g in range(3):
        w_sent(g)
    for k in range(8):
        b6(k).wait_send()
    for k in range(1, 8):

        @pl.when(y >= k)
        def _():
            q_copy(k).wait_send()

        @pl.when(y + k < NY)
        def _():
            o_copy(k).wait_send()

    for cp in (text_cp, e1, e2, e3):
        cp.wait_send()


def shards(
    patches,
    grid,
    vit_gain,
    vit_qkv,
    vit_out,
    merge_weight,
    text_embeds,
    prompt_pos,
    dec_gain,
    dec_qkv,
    dec_out,
):
    vm = pl.BlockSpec(memory_space=pltpu.VMEM)
    dma = pltpu.SemaphoreType.DMA
    scratch = [
        pltpu.VMEM((3, 2, NX, NY, 20, 640), BF),
        pltpu.VMEM((1280, 640), BF),
        pltpu.VMEM((640, 640), BF),
        pltpu.VMEM((1280, 640), BF),
        pltpu.VMEM((2, 1280, 128), F32),
        pltpu.VMEM((8, FEAT, 256), BF),
        pltpu.VMEM((8, FEAT, 256), BF),
        pltpu.VMEM((8, FEAT, 256), BF),
        pltpu.VMEM((256, 256), BF),
        pltpu.VMEM((2, FEAT, 256), BF),
        pltpu.VMEM((8, HALF, 128), BF),
        pltpu.VMEM((8, HALF, 128), BF),
        pltpu.VMEM((8, HALF, 128), BF),
        pltpu.VMEM((NX, ROWS, 1024), BF),
        pltpu.VMEM((16, ROWS), F32),
        pltpu.VMEM((2, 2, HALF, ROWS), BF),
        pltpu.VMEM((NX, HALF, ROWS), BF),
        pltpu.VMEM((NX, HALF, ROWS), BF),
        pltpu.VMEM((8, 2, HALF, ROWS), BF),
        pltpu.VMEM((NX, 160, ROWS), BF),
        pltpu.VMEM((NX, ROWS, 80), BF),
        pltpu.VMEM((8, 80, ROWS), BF),
        pltpu.VMEM((NX, ROWS, ROWS), F32),
        pltpu.VMEM((8, 96, ROWS), BF),
        pltpu.VMEM((8, 96, ROWS), BF),
        pltpu.VMEM((2, 80, ROWS), BF),
        pltpu.VMEM((8, HALF, ROWS), BF),
        pltpu.VMEM((8, HALF, ROWS), BF),
        pltpu.VMEM((2, HALF, ROWS), BF),
    ]
    sems = []
    for shape in ((5, 8), (3, 8), (3, 4), (3, 4), (8,), (4,), (8,), (8,), (4,), (8,), (4,)):
        sems += [dma(shape), dma(shape)]
    return pl.pallas_call(
        kernel,
        out_shape=jax.ShapeDtypeStruct((160, 160), BF),
        in_specs=[pl.BlockSpec(memory_space=pltpu.SMEM)] + [vm] * 10,
        out_specs=vm,
        scratch_shapes=scratch + sems,
        compiler_params=pltpu.CompilerParams(
            collective_id=0, has_side_effects=True, vmem_limit_bytes=60 << 20
        ),
        name="layer",
    )(
        grid,
        patches[0].T,
        vit_gain.reshape(10, 128),
        vit_qkv,
        vit_out.T,
        merge_weight.transpose(2, 0, 1),
        text_embeds,
        prompt_pos,
        dec_gain.reshape(10, 128),
        dec_qkv,
        dec_out.T,
    )


def solution(mesh):
    placed = (
        P("wide", None, "narrow"),
        P("wide", None),
        P(),
        P("wide", "narrow"),
        P("narrow", "wide"),
        P(None, "narrow", "wide"),
        P("wide", "narrow"),
        P(),
        P(),
        P("wide", "narrow"),
        P("narrow", "wide"),
    )
    return jax.shard_map(
        shards, mesh=mesh, in_specs=placed, out_specs=P("wide", "narrow"), check_vma=False
    )
```

```python
import functools

import jax
import jax.numpy as jnp
from jax import lax
from jax.experimental import pallas as pl
from jax.experimental.pallas import tpu as pltpu
from jax.sharding import PartitionSpec as P

HEAD = 80
SCALE = HEAD ** -0.5
EPS = 1e-6
NZ, NY, NX = 8, 8, 4
FEAT = 160
HALF = 80
ROWS = 320
BF = jnp.bfloat16
F32 = jnp.float32
MESH = pl.DeviceIdType.MESH
ORDER7 = (4, 3, 5, 2, 6, 1, 7)
NEAR7 = (1, 7, 2, 6, 3, 5, 4)
ORDER3 = (2, 1, 3)


def dg(a, b, ca, cb):
    return lax.dot_general(a, b, (((ca,), (cb,)), ((), ())), preferred_element_type=F32)


def iota(shape, axis):
    return lax.broadcasted_iota(jnp.int32, shape, axis)


def kernel(
    grid_ref,
    patches_ref,
    vgain_ref,
    vqkv_ref,
    vout_ref,
    merge_ref,
    text_ref,
    ppos_ref,
    dgain_ref,
    dqkv_ref,
    dout_ref,
    out_ref,
    wbuf,
    wa,
    wm,
    wc,
    gains,
    xz,
    az,
    own_out,
    zt,
    wo,
    imgs,
    p3,
    r3,
    mt,
    hot,
    seen,
    txt,
    route_s,
    route_r,
    dz,
    kv,
    kt,
    qb,
    sc,
    ob,
    orx,
    ad,
    fin,
    zs,
    zr,
    wys,
    wyr,
    wxs,
    wxr,
    wbs,
    wbr,
    y4s,
    y4r,
    x5s,
    x5r,
    b6s,
    b6r,
    q7s,
    q7r,
    k7s,
    k7r,
    o8s,
    o8r,
    sbs,
    sbr,
    oas,
    oar,
    oys,
    oyr,
    oxs,
    oxr,
    obs,
    obr,
    b9s,
    b9r,
):
    w = lax.axis_index("wide")
    z = lax.axis_index("narrow")
    y, x, c = w // 8, (w // 2) % 4, w % 2

    def dev(yy, xx, cc, zz):
        return (yy * 8 + xx * 2 + cc, zz)

    def zpeer(k):
        return dev(y, x, c, (z + k) % NZ)

    def ypeer(k):
        return dev((y + k) % NY, x, c, z)

    def xpeer(k):
        return dev(y, (x + k) % NX, c, z)

    sib = dev(y, x, 1 - c, z)

    def rcopy(src, dst, s, r, to):
        return pltpu.make_async_remote_copy(
            src_ref=src, dst_ref=dst, send_sem=s, recv_sem=r, device_id=to, device_id_type=MESH
        )

    barrier = pltpu.get_barrier_semaphore()
    peers = [zpeer(k) for k in range(1, 8)] + [ypeer(k) for k in range(1, 8)]
    peers += [xpeer(k) for k in range(1, 4)] + [sib]
    for p in peers:
        pl.semaphore_signal(barrier, inc=1, device_id=p, device_id_type=MESH)

    slot_to = iota((256, 256), 1)
    sub, tok = slot_to // 64, slot_to % 64
    want = (2 * (tok // 8) + sub // 2) * 16 + 2 * (tok % 8) + sub % 2
    perm = (iota((256, 256), 0) == want).astype(F32).astype(BF)
    xz[z] = dg(patches_ref[...], perm, 1, 0).astype(BF)

    pad = jnp.zeros((20, 32), BF)
    wbuf[0, c, x, y, :, :512] = jnp.concatenate([vqkv_ref[...], pad], axis=1)
    wbuf[1, c, x, y] = jnp.concatenate([merge_ref[:, j, :] for j in range(4)], axis=1)
    wbuf[2, c, x, y, :, :512] = jnp.concatenate([dqkv_ref[...], pad], axis=1)
    own_out[0] = vout_ref[...]
    own_out[1] = dout_ref[...]
    zt[z] = own_out[...]
    place = (iota((FEAT, ROWS), 1) == iota((FEAT, ROWS), 0) + FEAT * c).astype(F32).astype(BF)
    own_text = dg(text_ref[...], place, 0, 0).astype(BF)
    txt[0, 0] = own_text[:HALF]
    txt[0, 1] = own_text[HALF:]

    pl.semaphore_wait(barrier, len(peers))

    def z_gather(phase, buf):
        cps = {k: rcopy(buf, buf, zs.at[phase, k], zr.at[phase, k], zpeer(k)) for k in ORDER7}
        for k in ORDER7:
            cps[k].start()
        return cps

    p1 = z_gather(0, xz.at[z])

    def wide(g):
        return pl.ds(0, 640 if g == 1 else 512)

    def wy(g, k):
        ref = wbuf.at[g, c, x, y, :, wide(g)]
        return rcopy(ref, ref, wys.at[g, k], wyr.at[g, k], ypeer(k))

    def wx(g, k):
        ref = wbuf.at[g, c, x, :, :, wide(g)]
        return rcopy(ref, ref, wxs.at[g, k], wxr.at[g, k], xpeer(k))

    def wb(g, k):
        ref = wbuf.at[g, c, (x + NX - k) % NX, :, :, wide(g)]
        return rcopy(ref, ref, wbs.at[g, k], wbr.at[g, k], sib)

    def wx_piece(g, k, j):
        ref = wbuf.at[g, c, x, (y + NY - k) % NY, :, wide(g)]
        return rcopy(ref, ref, wxs.at[g, j], wxr.at[g, j], xpeer(j))

    def y_go(g):
        for k in NEAR7:
            wy(g, k).start()
        for j in ORDER3:
            wx_piece(g, 0, j).start()

    home = (z == y)
    apart = (y + NZ - z) % NZ

    def oa(k):
        return rcopy(own_out, zt.at[z], oas.at[k], oar.at[k], dev(y, x, c, y))

    def oy(k):
        ref = wo.at[c, x]
        return rcopy(ref, ref, oys.at[k], oyr.at[k], ypeer(k))

    def ox(j):
        ref = wo.at[c, x]
        return rcopy(ref, ref, oxs.at[j], oxr.at[j], xpeer(j))

    def o_sib(j):
        ref = wo.at[c, (x + NX - j) % NX]
        return rcopy(ref, ref, obs.at[j], obr.at[j], sib)

    @pl.when(jnp.logical_not(home))
    def _():
        oa(apart).start()

    y_go(0)
    text_cp = rcopy(txt.at[0, 1 - c], txt.at[1, 0], sbs.at[0], sbr.at[0], sib)
    text_cp.start()

    def y_done(g):
        for k in NEAR7:
            wy(g, k).wait_recv()
            for j in ORDER3:
                wx_piece(g, k, j).start()
        wb(g, 0).start()

    def x_done(g):
        for k in ORDER3:
            wx(g, k).wait_recv()
            wb(g, k).start()

    def b_done(g):
        for k in range(4):
            wb(g, k).wait_recv()

    def w_sent(g):
        for k in ORDER7:
            wy(g, k).wait_send()
        for k in ORDER3:
            wx(g, k).wait_send()
        for k in range(4):
            wb(g, k).wait_send()

    for k in range(10):
        at = slice(128 * k, 128 * k + 128)
        gains[0, at, :] = jnp.broadcast_to(vgain_ref[k : k + 1, :], (128, 128)).T
        gains[1, at, :] = jnp.broadcast_to(dgain_ref[k : k + 1, :], (128, 128)).T

    y_done(0)

    @pl.when(home)
    def _():
        for k in range(1, 8):
            rcopy(own_out, zt.at[(z + NZ - k) % NZ], oas.at[k], oar.at[k], zpeer(k)).wait_recv()
        for t in range(2):
            wo[c, x, t] = jnp.concatenate([zt[j, t] for j in range(8)], axis=1)
        for k in NEAR7:
            oy(k).start()

    y_go(1)

    def chip_tokens(j):
        return jnp.concatenate([ppos_ref[pl.ds(2 * j, 1), :], ppos_ref[pl.ds(2 * j + 1, 1), :]], axis=1)

    def table(t, carry):
        base = ROWS * (4 * y + t)
        rows = iota((ROWS, 128), 0) + base
        for j in range(NY):
            tokens = chip_tokens(4 * j + x)
            hot[t, :, 128 * j : 128 * j + 128] = (rows == tokens).astype(F32).astype(BF)
        return carry

    lax.fori_loop(0, NX, table, 0)

    mine = iota((ROWS, 128), 0) + ROWS * (4 * y + x)

    def mark(j, carry):
        return jnp.maximum(carry, (mine == chip_tokens(j)).astype(F32))

    hits = lax.fori_loop(0, 32, mark, jnp.zeros((ROWS, 128), F32)).astype(BF)
    seen[...] = dg(jnp.ones((16, 128), BF), hits, 1, 1)

    x_done(0)

    @pl.when(jnp.logical_not(home))
    def _():
        oy(apart).wait_recv()

    for j in ORDER3:
        ox(j).start()
    o_sib(0).start()
    y_done(1)
    y_go(2)
    b_done(0)

    def pieces(g, row):
        return [wbuf[g, cc, xx, row, :, :512] for xx in range(NX) for cc in range(2)]

    def build_a(row, carry):
        wa[pl.ds(pl.multiple_of(FEAT * row, 16), FEAT), :] = jnp.concatenate(pieces(0, row), axis=0)
        return carry

    lax.fori_loop(0, NY, build_a, 0)

    for k in ORDER7:
        p1[k].wait_recv()
    xa = xz[...].reshape(8 * FEAT, 256).astype(F32)
    mean = jnp.sum(xa, axis=0, keepdims=True) * (1.0 / 1280.0)
    xa = xa - mean
    var = jnp.sum(xa * xa, axis=0, keepdims=True) * (1.0 / 1280.0)
    gain = jnp.concatenate([gains[0], gains[0]], axis=1)
    normed = (xa * lax.rsqrt(var + EPS) * gain).astype(BF)
    proj = dg(wa[...], normed, 0, 0).astype(BF)
    slot = iota((256, 256), 0)
    sub, tok = slot // 64, slot % 64
    row_id = 2 * (tok // 8) + sub // 2
    col_id = 2 * (tok % 8) + sub % 2
    keep = (row_id < grid_ref[0, 0]) & (col_id < grid_ref[0, 1])
    for h in range(2):
        qh = proj[240 * h : 240 * h + 80]
        kh = proj[240 * h + 80 : 240 * h + 160]
        vh = proj[240 * h + 160 : 240 * h + 240]
        s = dg(kh, qh, 0, 0) * SCALE
        s = jnp.where(keep, s, -jnp.inf)
        p = jnp.exp(s - jnp.max(s, axis=0, keepdims=True))
        total = jnp.sum(p, axis=0, keepdims=True)
        o = dg(vh, p.astype(BF), 1, 0) / total
        az[z, 80 * h : 80 * h + 80] = o.astype(BF)

    def z_scatter(phase, src, dst):
        cps = {
            k: rcopy(src.at[(z + k) % NZ], dst.at[z], zs.at[phase, k], zr.at[phase, k], zpeer(k))
            for k in ORDER7
        }
        for k in ORDER7:
            cps[k].start()
        dst[z] = src[z]
        return cps

    def ring_of(phase, at, split, rows):
        def copy(right, s):
            block = (z + NZ - s) % NZ if right else (z + s) % NZ
            ref = at(block)
            if s == 3:
                ref = ref.at[pl.ds(0, split)] if right else ref.at[pl.ds(split, rows - split)]
            sem = s if right else 4 + s
            to = zpeer(1 if right else NZ - 1)
            return rcopy(ref, ref, zs.at[phase, sem], zr.at[phase, sem], to)

        return copy

    def ring_step(copy, s):
        copy(True, s).wait_recv()
        if s < 3:
            copy(True, s + 1).start()
        copy(False, s).wait_recv()
        if s < 3:
            copy(False, s + 1).start()

    p2 = ring_of(1, lambda j: az.at[j], 80, FEAT)
    p2(True, 0).start()
    p2(False, 0).start()

    ring_step(p2, 0)
    for j in ORDER3:
        ox(j).wait_recv()
        o_sib(j).start()
    ring_step(p2, 1)
    x_done(1)
    y_done(2)
    ring_step(p2, 2)
    ring_step(p2, 3)
    for j in range(4):
        o_sib(j).wait_recv()
    b_done(1)

    def build_m(row, carry):
        parts = [wbuf[1, cc, 2 * c + xx, row] for xx in range(2) for cc in range(2)]
        wm[pl.ds(pl.multiple_of(HALF * row, 16), HALF), :] = jnp.concatenate(parts, axis=0)
        return carry

    lax.fori_loop(0, NY, build_m, 0)

    def sum8(ref):
        total = ref[0].astype(F32)
        for j in range(1, 8):
            total = total + ref[j].astype(F32)
        return total

    w_out = jnp.concatenate([wo[cc, xx, 0] for xx in range(NX) for cc in range(2)], axis=0)
    branch = dg(w_out, az[...].reshape(1280, 256), 1, 0)
    after = (xz[z].astype(F32) + branch).astype(BF)
    imgs[c] = after
    e1 = rcopy(imgs.at[c], imgs.at[c], sbs.at[1], sbr.at[1], sib)
    e1.start()
    e1.wait_recv()
    first, second = imgs[0], imgs[1]
    left = iota((FEAT, 128), 1) < 64
    stack = []
    for t in range(2):
        a, b = first[:, 128 * t : 128 * t + 128], second[:, 128 * t : 128 * t + 128]
        stack.append(jnp.where(left, a, pltpu.roll(b, 64, 1)))
        stack.append(jnp.where(left, pltpu.roll(a, 64, 1), b))
    grouped = jnp.concatenate(stack, axis=0)
    p3[...] = dg(wm[...], grouped, 1, 0).astype(BF).reshape(8, HALF, 128)
    c3 = z_scatter(2, p3, r3)

    x_done(2)
    b_done(2)

    def build_c(row, carry):
        wc[pl.ds(pl.multiple_of(FEAT * row, 16), FEAT), :] = jnp.concatenate(pieces(2, row), axis=0)
        return carry

    lax.fori_loop(0, NY, build_c, 0)

    for k in ORDER7:
        c3[k].wait_recv()
    mt[y] = sum8(r3).astype(BF)
    c4 = {k: rcopy(mt.at[y], mt.at[y], y4s.at[k], y4r.at[k], ypeer(k)) for k in ORDER7}
    for k in ORDER7:
        c4[k].start()
    for k in ORDER7:
        c4[k].wait_recv()
    tokens = jnp.concatenate([mt[j] for j in range(8)], axis=1)

    def routed(t):
        return dg(tokens, hot[t], 1, 1).astype(BF)

    c5 = {}
    for k in ORDER3:
        to = (x + k) % NX
        route_s[k] = routed(to)
        c5[k] = rcopy(route_s.at[k], route_r.at[k], x5s.at[k], x5r.at[k], xpeer(k))
        c5[k].start()
    image = routed(x).astype(F32)
    text_cp.wait_recv()
    my_text = txt[0, c].astype(F32) + txt[1, 0].astype(F32)
    for k in ORDER3:
        c5[k].wait_recv()
        image = image + route_r[k].astype(F32)
    dec_in = jnp.where(seen[0:1, :] > 0.5, image, my_text)
    dz[z, c] = dec_in.astype(BF)

    ring = ring_of(3, lambda j: dz.at[j, c], 48, HALF)
    ring(True, 0).start()
    ring(False, 0).start()

    def b6(k):
        ref = dz.at[(z + NZ - k) % NZ, c]
        return rcopy(ref, ref, b6s.at[k], b6r.at[k], sib)

    b6(0).start()
    for s in range(4):
        ring_step(ring, s)
        if s < 3:
            b6(s + 1).start()
            b6(7 - s).start()
        else:
            b6(4).start()
    for k in range(8):
        b6(k).wait_recv()
    xd = dz[...].reshape(1280, ROWS).astype(F32)
    power = jnp.sum(xd * xd, axis=0, keepdims=True) * (1.0 / 1280.0)
    g1 = gains[1]
    gain = jnp.concatenate([g1, g1, g1[:, :64]], axis=1)
    normed = (xd * lax.rsqrt(power + EPS) * gain).astype(BF)
    proj = dg(wc[...], normed, 0, 0).astype(BF)
    proj = jnp.where(c == 0, proj[:240], proj[240:480])
    qb[y] = proj[:80]
    kv[x] = proj[80:240]

    def q_copy(k):
        ref = qb.at[y]
        return rcopy(ref, ref, q7s.at[k], q7r.at[k], dev((y + NY - k) % NY, x, c, z))

    c7 = {k: rcopy(kv.at[x], kv.at[x], k7s.at[k], k7r.at[k], xpeer(k)) for k in ORDER3}
    for k in ORDER3:
        c7[k].start()
    for k in range(1, 8):

        @pl.when(y >= k)
        def _():
            q_copy(k).start()

    for k in ORDER3:
        c7[k].wait_recv()
    for t in range(NX):
        kt[t] = kv[t, :80].astype(F32).T.astype(BF)

    def o_copy(k):
        return rcopy(ob.at[k], orx.at[y], o8s.at[k], o8r.at[k], dev((y + k) % NY, x, c, z))

    def q_block(k, carry):
        @pl.when(k > 0)
        def _():
            q_copy(k).wait_recv()

        q = qb[y + k]
        limit = 1280 * k + ROWS * x + iota((ROWS, ROWS), 1)
        best = jnp.full((1, ROWS), -jnp.inf, F32)
        for t in range(NX):
            s = dg(kt[t], q, 1, 0) * SCALE
            s = jnp.where(iota((ROWS, ROWS), 0) + ROWS * t <= limit, s, -jnp.inf)
            best = jnp.maximum(best, jnp.max(s, axis=0, keepdims=True))
            sc[t] = s
        total = jnp.zeros((1, ROWS), F32)
        o = jnp.zeros((80, ROWS), F32)
        for t in range(NX):
            p = jnp.exp(sc[t] - best)
            total = total + jnp.sum(p, axis=0, keepdims=True)
            o = o + dg(kv[t, 80:], p.astype(BF), 1, 0)
        ob[k, :80] = (o / total).astype(BF)
        lse = best + jnp.log(total)
        hi = lse.astype(BF).astype(F32)
        mid = (lse - hi).astype(BF).astype(F32)
        low = lse - hi - mid
        at = iota((16, ROWS), 0)
        rows = jnp.where(at == 0, hi, jnp.where(at == 1, mid, jnp.where(at == 2, low, 0.0)))
        ob[k, 80:] = rows.astype(BF)

        @pl.when(k > 0)
        def _():
            o_copy(k).start()

        return carry

    lax.fori_loop(0, NY - y, q_block, 0)
    orx[y] = ob[0]
    for k in range(1, 8):

        @pl.when(y >= k)
        def _():
            rcopy(ob.at[k], orx.at[y - k], o8s.at[k], o8r.at[k], ypeer(0 - k)).wait_recv()

    def lse_of(j):
        return jnp.sum(orx[j, 80:].astype(F32), axis=0, keepdims=True)

    peak = lax.fori_loop(0, y + 1, lambda j, m: jnp.maximum(m, lse_of(j)), jnp.full((1, ROWS), -jnp.inf, F32))

    def merge_part(j, carry):
        o, total = carry
        share = jnp.exp(lse_of(j) - peak)
        return o + orx[j, :80].astype(F32) * share, total + share

    o, total = lax.fori_loop(
        0, y + 1, merge_part, (jnp.zeros((80, ROWS), F32), jnp.zeros((1, ROWS), F32))
    )
    ad[z, c] = (o / total).astype(BF)
    p9 = ring_of(4, lambda j: ad.at[j, c], 48, HALF)
    p9(True, 0).start()
    p9(False, 0).start()

    def b9(k):
        ref = ad.at[(z + NZ - k) % NZ, c]
        return rcopy(ref, ref, b9s.at[k], b9r.at[k], sib)

    b9(0).start()
    for s in range(4):
        ring_step(p9, s)
        if s < 3:
            b9(s + 1).start()
            b9(7 - s).start()
        else:
            b9(4).start()
    w_out = jnp.concatenate([wo[cc, 2 * c + xx, 1] for xx in range(2) for cc in range(2)], axis=0)
    for k in range(8):
        b9(k).wait_recv()
    branch = dg(w_out, ad[...].reshape(1280, ROWS), 1, 0)
    fin[c] = (dz[z, c].astype(F32) + branch).astype(BF)
    e3 = rcopy(fin.at[c], fin.at[c], sbs.at[2], sbr.at[2], sib)
    e3.start()
    e3.wait_recv()
    out_ref[...] = dg(place, jnp.concatenate([fin[0], fin[1]], axis=0), 1, 1).astype(BF)

    for s in range(4):
        for copy in (p2, ring, p9):
            copy(True, s).wait_send()
            copy(False, s).wait_send()
        o_sib(s).wait_send()
    for j in ORDER3:
        ox(j).wait_send()

    @pl.when(home)
    def _():
        for k in range(1, 8):
            oy(k).wait_send()

    @pl.when(jnp.logical_not(home))
    def _():
        oa(apart).wait_send()

    for cps in (p1, c3, c4):
        for k in ORDER7:
            cps[k].wait_send()
    for cps in (c5, c7):
        for k in ORDER3:
            cps[k].wait_send()
    for g in range(3):
        w_sent(g)
    for k in range(8):
        b6(k).wait_send()
        b9(k).wait_send()
    for k in range(1, 8):

        @pl.when(y >= k)
        def _():
            q_copy(k).wait_send()

        @pl.when(y + k < NY)
        def _():
            o_copy(k).wait_send()

    for cp in (text_cp, e1, e3):
        cp.wait_send()


def shards(
    patches,
    grid,
    vit_gain,
    vit_qkv,
    vit_out,
    merge_weight,
    text_embeds,
    prompt_pos,
    dec_gain,
    dec_qkv,
    dec_out,
):
    vm = pl.BlockSpec(memory_space=pltpu.VMEM)
    dma = pltpu.SemaphoreType.DMA
    scratch = [
        pltpu.VMEM((3, 2, NX, NY, 20, 640), BF),
        pltpu.VMEM((1280, 512), BF),
        pltpu.VMEM((640, 640), BF),
        pltpu.VMEM((1280, 512), BF),
        pltpu.VMEM((2, 1280, 128), F32),
        pltpu.VMEM((8, FEAT, 256), BF),
        pltpu.VMEM((8, FEAT, 256), BF),
        pltpu.VMEM((2, 20, FEAT), BF),
        pltpu.VMEM((8, 2, 20, FEAT), BF),
        pltpu.VMEM((2, NX, 2, 20, 1280), BF),
        pltpu.VMEM((2, FEAT, 256), BF),
        pltpu.VMEM((8, HALF, 128), BF),
        pltpu.VMEM((8, HALF, 128), BF),
        pltpu.VMEM((8, HALF, 128), BF),
        pltpu.VMEM((NX, ROWS, 1024), BF),
        pltpu.VMEM((16, ROWS), F32),
        pltpu.VMEM((2, 2, HALF, ROWS), BF),
        pltpu.VMEM((NX, HALF, ROWS), BF),
        pltpu.VMEM((NX, HALF, ROWS), BF),
        pltpu.VMEM((8, 2, HALF, ROWS), BF),
        pltpu.VMEM((NX, 160, ROWS), BF),
        pltpu.VMEM((NX, ROWS, 80), BF),
        pltpu.VMEM((8, 80, ROWS), BF),
        pltpu.VMEM((NX, ROWS, ROWS), F32),
        pltpu.VMEM((8, 96, ROWS), BF),
        pltpu.VMEM((8, 96, ROWS), BF),
        pltpu.VMEM((8, 2, HALF, ROWS), BF),
        pltpu.VMEM((2, HALF, ROWS), BF),
    ]
    sems = []
    for shape in ((5, 8), (3, 8), (3, 4), (3, 4), (8,), (4,), (8,), (8,), (4,), (8,), (4,), (8,), (8,), (4,), (4,), (8,)):
        sems += [dma(shape), dma(shape)]
    return pl.pallas_call(
        kernel,
        out_shape=jax.ShapeDtypeStruct((160, 160), BF),
        in_specs=[pl.BlockSpec(memory_space=pltpu.SMEM)] + [vm] * 10,
        out_specs=vm,
        scratch_shapes=scratch + sems,
        compiler_params=pltpu.CompilerParams(
            collective_id=0, has_side_effects=True, vmem_limit_bytes=60 << 20
        ),
        name="layer",
    )(
        grid,
        patches[0].T,
        vit_gain.reshape(10, 128),
        vit_qkv,
        vit_out.T,
        merge_weight.transpose(2, 0, 1),
        text_embeds,
        prompt_pos,
        dec_gain.reshape(10, 128),
        dec_qkv,
        dec_out.T,
    )


def solution(mesh):
    placed = (
        P("wide", None, "narrow"),
        P("wide", None),
        P(),
        P("wide", "narrow"),
        P("narrow", "wide"),
        P(None, "narrow", "wide"),
        P("wide", "narrow"),
        P(),
        P(),
        P("wide", "narrow"),
        P("narrow", "wide"),
    )
    return jax.shard_map(
        shards, mesh=mesh, in_specs=placed, out_specs=P("wide", "narrow"), check_vma=False
    )
```

```python
import functools

import jax
import jax.numpy as jnp
from jax import lax
from jax.experimental import pallas as pl
from jax.experimental.pallas import tpu as pltpu
from jax.sharding import PartitionSpec as P

HEAD = 80
SCALE = HEAD ** -0.5
EPS = 1e-6
NZ, NY, NX = 8, 8, 4
FEAT = 160
HALF = 80
ROWS = 320
BF = jnp.bfloat16
F32 = jnp.float32
MESH = pl.DeviceIdType.MESH
ORDER7 = (4, 3, 5, 2, 6, 1, 7)
NEAR7 = (1, 7, 2, 6, 3, 5, 4)
ORDER3 = (2, 1, 3)


def dg(a, b, ca, cb):
    return lax.dot_general(a, b, (((ca,), (cb,)), ((), ())), preferred_element_type=F32)


def iota(shape, axis):
    return lax.broadcasted_iota(jnp.int32, shape, axis)


def kernel(
    grid_ref,
    patches_ref,
    vgain_ref,
    vqkv_ref,
    vout_ref,
    merge_ref,
    text_ref,
    ppos_ref,
    dgain_ref,
    dqkv_ref,
    dout_ref,
    out_ref,
    wbuf,
    wa,
    wm,
    wc,
    gains,
    xz,
    pz,
    rz,
    att,
    imgs,
    p3,
    r3,
    mt,
    hot,
    seen,
    txt,
    route_s,
    route_r,
    dz,
    kv,
    kt,
    qb,
    sc,
    ob,
    orx,
    attd,
    p9,
    r9,
    fin,
    zs,
    zr,
    wys,
    wyr,
    wxs,
    wxr,
    wbs,
    wbr,
    y4s,
    y4r,
    x5s,
    x5r,
    b6s,
    b6r,
    q7s,
    q7r,
    k7s,
    k7r,
    o8s,
    o8r,
    sbs,
    sbr,
):
    w = lax.axis_index("wide")
    z = lax.axis_index("narrow")
    y, x, c = w // 8, (w // 2) % 4, w % 2

    def dev(yy, xx, cc, zz):
        return (yy * 8 + xx * 2 + cc, zz)

    def zpeer(k):
        return dev(y, x, c, (z + k) % NZ)

    def ypeer(k):
        return dev((y + k) % NY, x, c, z)

    def xpeer(k):
        return dev(y, (x + k) % NX, c, z)

    sib = dev(y, x, 1 - c, z)

    def rcopy(src, dst, s, r, to):
        return pltpu.make_async_remote_copy(
            src_ref=src, dst_ref=dst, send_sem=s, recv_sem=r, device_id=to, device_id_type=MESH
        )

    barrier = pltpu.get_barrier_semaphore()
    peers = [zpeer(k) for k in range(1, 8)] + [ypeer(k) for k in range(1, 8)]
    peers += [xpeer(k) for k in range(1, 4)] + [sib]
    for p in peers:
        pl.semaphore_signal(barrier, inc=1, device_id=p, device_id_type=MESH)

    slot_to = iota((256, 256), 1)
    sub, tok = slot_to // 64, slot_to % 64
    want = (2 * (tok // 8) + sub // 2) * 16 + 2 * (tok % 8) + sub % 2
    perm = (iota((256, 256), 0) == want).astype(F32).astype(BF)
    xz[z] = dg(patches_ref[...], perm, 1, 0).astype(BF)

    wbuf[0, c, x, y] = jnp.concatenate([vqkv_ref[...], vout_ref[...]], axis=1)
    wbuf[1, c, x, y] = jnp.concatenate([merge_ref[:, j, :] for j in range(4)], axis=1)
    wbuf[2, c, x, y] = jnp.concatenate([dqkv_ref[...], dout_ref[...]], axis=1)
    place = (iota((FEAT, ROWS), 1) == iota((FEAT, ROWS), 0) + FEAT * c).astype(F32).astype(BF)
    own_text = dg(text_ref[...], place, 0, 0).astype(BF)
    txt[0, 0] = own_text[:HALF]
    txt[0, 1] = own_text[HALF:]

    pl.semaphore_wait(barrier, len(peers))

    def z_gather(phase, buf):
        cps = {k: rcopy(buf, buf, zs.at[phase, k], zr.at[phase, k], zpeer(k)) for k in ORDER7}
        for k in ORDER7:
            cps[k].start()
        return cps

    p1 = z_gather(0, xz.at[z])

    def wy(g, k):
        ref = wbuf.at[g, c, x, y]
        return rcopy(ref, ref, wys.at[g, k], wyr.at[g, k], ypeer(k))

    def wx(g, k):
        ref = wbuf.at[g, c, x]
        return rcopy(ref, ref, wxs.at[g, k], wxr.at[g, k], xpeer(k))

    def wb(g, k):
        ref = wbuf.at[g, c, (x + NX - k) % NX]
        return rcopy(ref, ref, wbs.at[g, k], wbr.at[g, k], sib)

    def wx_piece(g, k, j):
        ref = wbuf.at[g, c, x, (y + NY - k) % NY]
        return rcopy(ref, ref, wxs.at[g, j], wxr.at[g, j], xpeer(j))

    def y_go(g):
        for k in NEAR7:
            wy(g, k).start()
        for j in ORDER3:
            wx_piece(g, 0, j).start()

    y_go(0)
    text_cp = rcopy(txt.at[0, 1 - c], txt.at[1, 0], sbs.at[0], sbr.at[0], sib)
    text_cp.start()

    def y_done(g):
        for k in NEAR7:
            wy(g, k).wait_recv()
            for j in ORDER3:
                wx_piece(g, k, j).start()
        wb(g, 0).start()

    def x_done(g):
        for k in ORDER3:
            wx(g, k).wait_recv()
            wb(g, k).start()

    def b_done(g):
        for k in range(4):
            wb(g, k).wait_recv()

    def w_sent(g):
        for k in ORDER7:
            wy(g, k).wait_send()
        for k in ORDER3:
            wx(g, k).wait_send()
        for k in range(4):
            wb(g, k).wait_send()

    for k in range(10):
        at = slice(128 * k, 128 * k + 128)
        gains[0, at, :] = jnp.broadcast_to(vgain_ref[k : k + 1, :], (128, 128)).T
        gains[1, at, :] = jnp.broadcast_to(dgain_ref[k : k + 1, :], (128, 128)).T

    y_done(0)
    y_go(1)

    def chip_tokens(j):
        return jnp.concatenate([ppos_ref[pl.ds(2 * j, 1), :], ppos_ref[pl.ds(2 * j + 1, 1), :]], axis=1)

    def table(t, carry):
        base = ROWS * (4 * y + t)
        rows = iota((ROWS, 128), 0) + base
        for j in range(NY):
            tokens = chip_tokens(4 * j + x)
            hot[t, :, 128 * j : 128 * j + 128] = (rows == tokens).astype(F32).astype(BF)
        return carry

    lax.fori_loop(0, NX, table, 0)

    mine = iota((ROWS, 128), 0) + ROWS * (4 * y + x)

    def mark(j, carry):
        return jnp.maximum(carry, (mine == chip_tokens(j)).astype(F32))

    hits = lax.fori_loop(0, 32, mark, jnp.zeros((ROWS, 128), F32)).astype(BF)
    seen[...] = dg(jnp.ones((16, 128), BF), hits, 1, 1)

    x_done(0)
    y_done(1)
    y_go(2)
    b_done(0)

    def pieces(g, row):
        return [wbuf[g, cc, xx, row] for xx in range(NX) for cc in range(2)]

    def build_a(row, carry):
        wa[pl.ds(pl.multiple_of(FEAT * row, 16), FEAT), :] = jnp.concatenate(pieces(0, row), axis=0)
        return carry

    lax.fori_loop(0, NY, build_a, 0)

    for k in ORDER7:
        p1[k].wait_recv()
    xa = xz[...].reshape(8 * FEAT, 256).astype(F32)
    mean = jnp.sum(xa, axis=0, keepdims=True) * (1.0 / 1280.0)
    xa = xa - mean
    var = jnp.sum(xa * xa, axis=0, keepdims=True) * (1.0 / 1280.0)
    gain = jnp.concatenate([gains[0], gains[0]], axis=1)
    normed = (xa * lax.rsqrt(var + EPS) * gain).astype(BF)
    proj = dg(wa[:, :512], normed, 0, 0).astype(BF)
    slot = iota((256, 256), 0)
    sub, tok = slot // 64, slot % 64
    row_id = 2 * (tok // 8) + sub // 2
    col_id = 2 * (tok % 8) + sub % 2
    keep = (row_id < grid_ref[0, 0]) & (col_id < grid_ref[0, 1])
    att[0:96] = jnp.zeros((96, 256), BF)
    for h in range(2):
        qh = proj[240 * h : 240 * h + 80]
        kh = proj[240 * h + 80 : 240 * h + 160]
        vh = proj[240 * h + 160 : 240 * h + 240]
        s = dg(kh, qh, 0, 0) * SCALE
        s = jnp.where(keep, s, -jnp.inf)
        p = jnp.exp(s - jnp.max(s, axis=0, keepdims=True))
        total = jnp.sum(p, axis=0, keepdims=True)
        o = dg(vh, p.astype(BF), 1, 0) / total
        att[96 + 80 * h : 176 + 80 * h] = o.astype(BF)
    pz[...] = dg(wa[:, 384:640], att[...], 1, 0).astype(BF).reshape(8, FEAT, 256)

    def z_scatter(phase, src, dst):
        cps = {
            k: rcopy(src.at[(z + k) % NZ], dst.at[z], zs.at[phase, k], zr.at[phase, k], zpeer(k))
            for k in ORDER7
        }
        for k in ORDER7:
            cps[k].start()
        dst[z] = src[z]
        return cps

    p2 = z_scatter(1, pz, rz)

    x_done(1)
    y_done(2)
    b_done(1)

    def build_m(row, carry):
        parts = [wbuf[1, cc, 2 * c + xx, row] for xx in range(2) for cc in range(2)]
        wm[pl.ds(pl.multiple_of(HALF * row, 16), HALF), :] = jnp.concatenate(parts, axis=0)
        return carry

    lax.fori_loop(0, NY, build_m, 0)

    def sum8(ref):
        total = ref[0].astype(F32)
        for j in range(1, 8):
            total = total + ref[j].astype(F32)
        return total

    for k in ORDER7:
        p2[k].wait_recv()
    after = (xz[z].astype(F32) + sum8(rz)).astype(BF)
    imgs[c] = after
    e1 = rcopy(imgs.at[c], imgs.at[c], sbs.at[1], sbr.at[1], sib)
    e1.start()
    e1.wait_recv()
    first, second = imgs[0], imgs[1]
    left = iota((FEAT, 128), 1) < 64
    stack = []
    for t in range(2):
        a, b = first[:, 128 * t : 128 * t + 128], second[:, 128 * t : 128 * t + 128]
        stack.append(jnp.where(left, a, pltpu.roll(b, 64, 1)))
        stack.append(jnp.where(left, pltpu.roll(a, 64, 1), b))
    grouped = jnp.concatenate(stack, axis=0)
    p3[...] = dg(wm[...], grouped, 1, 0).astype(BF).reshape(8, HALF, 128)
    c3 = z_scatter(2, p3, r3)

    x_done(2)
    b_done(2)

    def build_c(row, carry):
        wc[pl.ds(pl.multiple_of(FEAT * row, 16), FEAT), :] = jnp.concatenate(pieces(2, row), axis=0)
        return carry

    lax.fori_loop(0, NY, build_c, 0)

    for k in ORDER7:
        c3[k].wait_recv()
    mt[y] = sum8(r3).astype(BF)
    c4 = {k: rcopy(mt.at[y], mt.at[y], y4s.at[k], y4r.at[k], ypeer(k)) for k in ORDER7}
    for k in ORDER7:
        c4[k].start()
    for k in ORDER7:
        c4[k].wait_recv()
    tokens = jnp.concatenate([mt[j] for j in range(8)], axis=1)

    def routed(t):
        return dg(tokens, hot[t], 1, 1).astype(BF)

    c5 = {}
    for k in ORDER3:
        to = (x + k) % NX
        route_s[k] = routed(to)
        c5[k] = rcopy(route_s.at[k], route_r.at[k], x5s.at[k], x5r.at[k], xpeer(k))
        c5[k].start()
    image = routed(x).astype(F32)
    text_cp.wait_recv()
    my_text = txt[0, c].astype(F32) + txt[1, 0].astype(F32)
    for k in ORDER3:
        c5[k].wait_recv()
        image = image + route_r[k].astype(F32)
    dec_in = jnp.where(seen[0:1, :] > 0.5, image, my_text)
    dz[z, c] = dec_in.astype(BF)

    p6 = z_gather(3, dz.at[z, c])

    def b6(k):
        ref = dz.at[(z + NZ - k) % NZ, c]
        return rcopy(ref, ref, b6s.at[k], b6r.at[k], sib)

    b6(0).start()
    for k in ORDER7:
        p6[k].wait_recv()
        b6(k).start()
    for k in range(8):
        b6(k).wait_recv()
    xd = dz[...].reshape(1280, ROWS).astype(F32)
    power = jnp.sum(xd * xd, axis=0, keepdims=True) * (1.0 / 1280.0)
    g1 = gains[1]
    gain = jnp.concatenate([g1, g1, g1[:, :64]], axis=1)
    normed = (xd * lax.rsqrt(power + EPS) * gain).astype(BF)
    proj = dg(wc[:, :512], normed, 0, 0).astype(BF)
    proj = jnp.where(c == 0, proj[:240], proj[240:480])
    qb[y] = proj[:80]
    kv[x] = proj[80:240]

    def q_copy(k):
        ref = qb.at[y]
        return rcopy(ref, ref, q7s.at[k], q7r.at[k], dev((y + NY - k) % NY, x, c, z))

    c7 = {k: rcopy(kv.at[x], kv.at[x], k7s.at[k], k7r.at[k], xpeer(k)) for k in ORDER3}
    for k in ORDER3:
        c7[k].start()
    for k in range(1, 8):

        @pl.when(y >= k)
        def _():
            q_copy(k).start()

    for k in ORDER3:
        c7[k].wait_recv()
    for t in range(NX):
        kt[t] = kv[t, :80].astype(F32).T.astype(BF)

    def o_copy(k):
        return rcopy(ob.at[k], orx.at[y], o8s.at[k], o8r.at[k], dev((y + k) % NY, x, c, z))

    def q_block(k, carry):
        @pl.when(k > 0)
        def _():
            q_copy(k).wait_recv()

        q = qb[y + k]
        limit = 1280 * k + ROWS * x + iota((ROWS, ROWS), 1)
        best = jnp.full((1, ROWS), -jnp.inf, F32)
        for t in range(NX):
            s = dg(kt[t], q, 1, 0) * SCALE
            s = jnp.where(iota((ROWS, ROWS), 0) + ROWS * t <= limit, s, -jnp.inf)
            best = jnp.maximum(best, jnp.max(s, axis=0, keepdims=True))
            sc[t] = s
        total = jnp.zeros((1, ROWS), F32)
        o = jnp.zeros((80, ROWS), F32)
        for t in range(NX):
            p = jnp.exp(sc[t] - best)
            total = total + jnp.sum(p, axis=0, keepdims=True)
            o = o + dg(kv[t, 80:], p.astype(BF), 1, 0)
        ob[k, :80] = (o / total).astype(BF)
        lse = best + jnp.log(total)
        hi = lse.astype(BF).astype(F32)
        mid = (lse - hi).astype(BF).astype(F32)
        low = lse - hi - mid
        at = iota((8, ROWS), 0)
        rows = jnp.where(at == 0, hi, jnp.where(at == 1, mid, jnp.where(at == 2, low, 0.0)))
        ob[k, 80:] = rows.astype(BF)

        @pl.when(k > 0)
        def _():
            o_copy(k).start()

        return carry

    lax.fori_loop(0, NY - y, q_block, 0)
    orx[y] = ob[0]
    for k in range(1, 8):

        @pl.when(y >= k)
        def _():
            rcopy(ob.at[k], orx.at[y - k], o8s.at[k], o8r.at[k], ypeer(0 - k)).wait_recv()

    def lse_of(j):
        return jnp.sum(orx[j, 80:].astype(F32), axis=0, keepdims=True)

    peak = lax.fori_loop(0, y + 1, lambda j, m: jnp.maximum(m, lse_of(j)), jnp.full((1, ROWS), -jnp.inf, F32))

    def merge_part(j, carry):
        o, total = carry
        share = jnp.exp(lse_of(j) - peak)
        return o + orx[j, :80].astype(F32) * share, total + share

    o, total = lax.fori_loop(
        0, y + 1, merge_part, (jnp.zeros((80, ROWS), F32), jnp.zeros((1, ROWS), F32))
    )
    attd[c] = (o / total).astype(BF)
    e2 = rcopy(attd.at[c], attd.at[c], sbs.at[2], sbr.at[2], sib)
    e2.start()
    e2.wait_recv()
    both = jnp.concatenate([jnp.zeros((96, ROWS), BF), attd[0], attd[1]], axis=0)
    for j in range(8):
        rows = wc[pl.ds(pl.multiple_of(FEAT * j + HALF * c, 16), HALF), 384:640]
        p9[j] = dg(rows, both, 1, 0).astype(BF)
    c9 = z_scatter(4, p9, r9)
    for k in ORDER7:
        c9[k].wait_recv()
    fin[c] = (dz[z, c].astype(F32) + sum8(r9)).astype(BF)
    e3 = rcopy(fin.at[c], fin.at[c], sbs.at[3], sbr.at[3], sib)
    e3.start()
    e3.wait_recv()
    out_ref[...] = dg(place, jnp.concatenate([fin[0], fin[1]], axis=0), 1, 1).astype(BF)

    for cps in (p1, p2, c3, c4, p6, c9):
        for k in ORDER7:
            cps[k].wait_send()
    for cps in (c5, c7):
        for k in ORDER3:
            cps[k].wait_send()
    for g in range(3):
        w_sent(g)
    for k in range(8):
        b6(k).wait_send()
    for k in range(1, 8):

        @pl.when(y >= k)
        def _():
            q_copy(k).wait_send()

        @pl.when(y + k < NY)
        def _():
            o_copy(k).wait_send()

    for cp in (text_cp, e1, e2, e3):
        cp.wait_send()


def shards(
    patches,
    grid,
    vit_gain,
    vit_qkv,
    vit_out,
    merge_weight,
    text_embeds,
    prompt_pos,
    dec_gain,
    dec_qkv,
    dec_out,
):
    vm = pl.BlockSpec(memory_space=pltpu.VMEM)
    dma = pltpu.SemaphoreType.DMA
    scratch = [
        pltpu.VMEM((3, 2, NX, NY, 20, 640), BF),
        pltpu.VMEM((1280, 640), BF),
        pltpu.VMEM((640, 640), BF),
        pltpu.VMEM((1280, 640), BF),
        pltpu.VMEM((2, 1280, 128), F32),
        pltpu.VMEM((8, FEAT, 256), BF),
        pltpu.VMEM((8, FEAT, 256), BF),
        pltpu.VMEM((8, FEAT, 256), BF),
        pltpu.VMEM((256, 256), BF),
        pltpu.VMEM((2, FEAT, 256), BF),
        pltpu.VMEM((8, HALF, 128), BF),
        pltpu.VMEM((8, HALF, 128), BF),
        pltpu.VMEM((8, HALF, 128), BF),
        pltpu.VMEM((NX, ROWS, 1024), BF),
        pltpu.VMEM((16, ROWS), F32),
        pltpu.VMEM((2, 2, HALF, ROWS), BF),
        pltpu.VMEM((NX, HALF, ROWS), BF),
        pltpu.VMEM((NX, HALF, ROWS), BF),
        pltpu.VMEM((8, 2, HALF, ROWS), BF),
        pltpu.VMEM((NX, 160, ROWS), BF),
        pltpu.VMEM((NX, ROWS, 80), BF),
        pltpu.VMEM((8, 80, ROWS), BF),
        pltpu.VMEM((NX, ROWS, ROWS), F32),
        pltpu.VMEM((8, 88, ROWS), BF),
        pltpu.VMEM((8, 88, ROWS), BF),
        pltpu.VMEM((2, 80, ROWS), BF),
        pltpu.VMEM((8, HALF, ROWS), BF),
        pltpu.VMEM((8, HALF, ROWS), BF),
        pltpu.VMEM((2, HALF, ROWS), BF),
    ]
    sems = []
    for shape in ((5, 8), (3, 8), (3, 4), (3, 4), (8,), (4,), (8,), (8,), (4,), (8,), (4,)):
        sems += [dma(shape), dma(shape)]
    return pl.pallas_call(
        kernel,
        out_shape=jax.ShapeDtypeStruct((160, 160), BF),
        in_specs=[pl.BlockSpec(memory_space=pltpu.SMEM)] + [vm] * 10,
        out_specs=vm,
        scratch_shapes=scratch + sems,
        compiler_params=pltpu.CompilerParams(
            collective_id=0, has_side_effects=True, vmem_limit_bytes=60 << 20
        ),
        name="layer",
    )(
        grid,
        patches[0].T,
        vit_gain.reshape(10, 128),
        vit_qkv,
        vit_out.T,
        merge_weight.transpose(2, 0, 1),
        text_embeds,
        prompt_pos,
        dec_gain.reshape(10, 128),
        dec_qkv,
        dec_out.T,
    )


def solution(mesh):
    placed = (
        P("wide", None, "narrow"),
        P("wide", None),
        P(),
        P("wide", "narrow"),
        P("narrow", "wide"),
        P(None, "narrow", "wide"),
        P("wide", "narrow"),
        P(),
        P(),
        P("wide", "narrow"),
        P("narrow", "wide"),
    )
    return jax.shard_map(
        shards, mesh=mesh, in_specs=placed, out_specs=P("wide", "narrow"), check_vma=False
    )
```

```python
import functools

import jax
import jax.numpy as jnp
from jax import lax
from jax.experimental import pallas as pl
from jax.experimental.pallas import tpu as pltpu
from jax.sharding import PartitionSpec as P

HEAD = 80
SCALE = HEAD ** -0.5
EPS = 1e-6
NZ, NY, NX = 8, 8, 4
FEAT = 160
HALF = 80
ROWS = 320
BF = jnp.bfloat16
F32 = jnp.float32
MESH = pl.DeviceIdType.MESH
ORDER7 = (4, 3, 5, 2, 6, 1, 7)
NEAR7 = (1, 7, 2, 6, 3, 5, 4)
ORDER3 = (2, 1, 3)


def dg(a, b, ca, cb):
    return lax.dot_general(a, b, (((ca,), (cb,)), ((), ())), preferred_element_type=F32)


def iota(shape, axis):
    return lax.broadcasted_iota(jnp.int32, shape, axis)


def kernel(
    grid_ref,
    patches_ref,
    vgain_ref,
    vqkv_ref,
    vout_ref,
    merge_ref,
    text_ref,
    ppos_ref,
    dgain_ref,
    dqkv_ref,
    dout_ref,
    out_ref,
    wbuf,
    wa,
    wm,
    wc,
    gains,
    xz,
    pz,
    rz,
    att,
    imgs,
    p3,
    r3,
    mt,
    hot,
    seen,
    txt,
    route_s,
    route_r,
    dz,
    kv,
    kt,
    qb,
    sc,
    ob,
    orx,
    attd,
    p9,
    r9,
    fin,
    zs,
    zr,
    wys,
    wyr,
    wxs,
    wxr,
    wbs,
    wbr,
    y4s,
    y4r,
    x5s,
    x5r,
    b6s,
    b6r,
    q7s,
    q7r,
    k7s,
    k7r,
    o8s,
    o8r,
    sbs,
    sbr,
):
    w = lax.axis_index("wide")
    z = lax.axis_index("narrow")
    y, x, c = w // 8, (w // 2) % 4, w % 2

    def dev(yy, xx, cc, zz):
        return (yy * 8 + xx * 2 + cc, zz)

    def zpeer(k):
        return dev(y, x, c, (z + k) % NZ)

    def ypeer(k):
        return dev((y + k) % NY, x, c, z)

    def xpeer(k):
        return dev(y, (x + k) % NX, c, z)

    sib = dev(y, x, 1 - c, z)

    def rcopy(src, dst, s, r, to):
        return pltpu.make_async_remote_copy(
            src_ref=src, dst_ref=dst, send_sem=s, recv_sem=r, device_id=to, device_id_type=MESH
        )

    barrier = pltpu.get_barrier_semaphore()
    peers = [zpeer(k) for k in range(1, 8)] + [ypeer(k) for k in range(1, 8)]
    peers += [xpeer(k) for k in range(1, 4)] + [sib]
    for p in peers:
        pl.semaphore_signal(barrier, inc=1, device_id=p, device_id_type=MESH)

    slot_to = iota((256, 256), 1)
    sub, tok = slot_to // 64, slot_to % 64
    want = (2 * (tok // 8) + sub // 2) * 16 + 2 * (tok % 8) + sub % 2
    perm = (iota((256, 256), 0) == want).astype(F32).astype(BF)
    xz[z] = dg(patches_ref[...], perm, 1, 0).astype(BF)

    wbuf[0, c, x, y] = jnp.concatenate([vqkv_ref[...], vout_ref[...]], axis=1)
    wbuf[1, c, x, y] = jnp.concatenate([merge_ref[:, j, :] for j in range(4)], axis=1)
    wbuf[2, c, x, y] = jnp.concatenate([dqkv_ref[...], dout_ref[...]], axis=1)
    place = (iota((FEAT, ROWS), 1) == iota((FEAT, ROWS), 0) + FEAT * c).astype(F32).astype(BF)
    own_text = dg(text_ref[...], place, 0, 0).astype(BF)
    txt[0, 0] = own_text[:HALF]
    txt[0, 1] = own_text[HALF:]

    pl.semaphore_wait(barrier, len(peers))

    def z_gather(phase, buf):
        cps = {k: rcopy(buf, buf, zs.at[phase, k], zr.at[phase, k], zpeer(k)) for k in ORDER7}
        for k in ORDER7:
            cps[k].start()
        return cps

    p1 = z_gather(0, xz.at[z])

    def wy(g, k):
        ref = wbuf.at[g, c, x, y]
        return rcopy(ref, ref, wys.at[g, k], wyr.at[g, k], ypeer(k))

    def wx(g, k):
        ref = wbuf.at[g, c, x]
        return rcopy(ref, ref, wxs.at[g, k], wxr.at[g, k], xpeer(k))

    def wb(g, k):
        ref = wbuf.at[g, c, (x + NX - k) % NX]
        return rcopy(ref, ref, wbs.at[g, k], wbr.at[g, k], sib)

    def wx_piece(g, k, j):
        ref = wbuf.at[g, c, x, (y + NY - k) % NY]
        return rcopy(ref, ref, wxs.at[g, j], wxr.at[g, j], xpeer(j))

    def y_go(g):
        for k in NEAR7:
            wy(g, k).start()
        for j in ORDER3:
            wx_piece(g, 0, j).start()

    y_go(0)
    text_cp = rcopy(txt.at[0, 1 - c], txt.at[1, 0], sbs.at[0], sbr.at[0], sib)
    text_cp.start()

    def y_done(g):
        for k in NEAR7:
            wy(g, k).wait_recv()
            for j in ORDER3:
                wx_piece(g, k, j).start()
        wb(g, 0).start()

    def x_done(g):
        for k in ORDER3:
            wx(g, k).wait_recv()
            wb(g, k).start()

    def b_done(g):
        for k in range(4):
            wb(g, k).wait_recv()

    def w_sent(g):
        for k in ORDER7:
            wy(g, k).wait_send()
        for k in ORDER3:
            wx(g, k).wait_send()
        for k in range(4):
            wb(g, k).wait_send()

    for k in range(10):
        at = slice(128 * k, 128 * k + 128)
        gains[0, at, :] = jnp.broadcast_to(vgain_ref[k : k + 1, :], (128, 128)).T
        gains[1, at, :] = jnp.broadcast_to(dgain_ref[k : k + 1, :], (128, 128)).T

    y_done(0)
    y_go(1)

    def chip_tokens(j):
        return jnp.concatenate([ppos_ref[pl.ds(2 * j, 1), :], ppos_ref[pl.ds(2 * j + 1, 1), :]], axis=1)

    def table(t, carry):
        base = ROWS * (4 * y + t)
        rows = iota((ROWS, 128), 0) + base
        for j in range(NY):
            tokens = chip_tokens(4 * j + x)
            hot[t, :, 128 * j : 128 * j + 128] = (rows == tokens).astype(F32).astype(BF)
        return carry

    lax.fori_loop(0, NX, table, 0)

    mine = iota((ROWS, 128), 0) + ROWS * (4 * y + x)

    def mark(j, carry):
        return jnp.maximum(carry, (mine == chip_tokens(j)).astype(F32))

    hits = lax.fori_loop(0, 32, mark, jnp.zeros((ROWS, 128), F32)).astype(BF)
    seen[...] = dg(jnp.ones((16, 128), BF), hits, 1, 1)

    x_done(0)
    y_done(1)
    y_go(2)
    b_done(0)

    def pieces(g, row):
        return [wbuf[g, cc, xx, row] for xx in range(NX) for cc in range(2)]

    def build_a(row, carry):
        wa[pl.ds(pl.multiple_of(FEAT * row, 16), FEAT), :] = jnp.concatenate(pieces(0, row), axis=0)
        return carry

    lax.fori_loop(0, NY, build_a, 0)

    for k in ORDER7:
        p1[k].wait_recv()
    xa = xz[...].reshape(8 * FEAT, 256).astype(F32)
    mean = jnp.sum(xa, axis=0, keepdims=True) * (1.0 / 1280.0)
    xa = xa - mean
    var = jnp.sum(xa * xa, axis=0, keepdims=True) * (1.0 / 1280.0)
    gain = jnp.concatenate([gains[0], gains[0]], axis=1)
    normed = (xa * lax.rsqrt(var + EPS) * gain).astype(BF)
    proj = dg(wa[:, :512], normed, 0, 0).astype(BF)
    slot = iota((256, 256), 0)
    sub, tok = slot // 64, slot % 64
    row_id = 2 * (tok // 8) + sub // 2
    col_id = 2 * (tok % 8) + sub % 2
    keep = (row_id < grid_ref[0, 0]) & (col_id < grid_ref[0, 1])
    att[0:96] = jnp.zeros((96, 256), BF)
    for h in range(2):
        qh = proj[240 * h : 240 * h + 80]
        kh = proj[240 * h + 80 : 240 * h + 160]
        vh = proj[240 * h + 160 : 240 * h + 240]
        s = dg(kh, qh, 0, 0) * SCALE
        s = jnp.where(keep, s, -jnp.inf)
        p = jnp.exp(s - jnp.max(s, axis=0, keepdims=True))
        total = jnp.sum(p, axis=0, keepdims=True)
        o = dg(vh, p.astype(BF), 1, 0) / total
        att[96 + 80 * h : 176 + 80 * h] = o.astype(BF)
    pz[...] = dg(wa[:, 384:640], att[...], 1, 0).astype(BF).reshape(8, FEAT, 256)

    def z_scatter(phase, src, dst):
        cps = {
            k: rcopy(src.at[(z + k) % NZ], dst.at[z], zs.at[phase, k], zr.at[phase, k], zpeer(k))
            for k in ORDER7
        }
        for k in ORDER7:
            cps[k].start()
        dst[z] = src[z]
        return cps

    p2 = z_scatter(1, pz, rz)

    x_done(1)
    y_done(2)
    b_done(1)

    def build_m(row, carry):
        parts = [wbuf[1, cc, 2 * c + xx, row] for xx in range(2) for cc in range(2)]
        wm[pl.ds(pl.multiple_of(HALF * row, 16), HALF), :] = jnp.concatenate(parts, axis=0)
        return carry

    lax.fori_loop(0, NY, build_m, 0)

    def sum8(ref):
        total = ref[0].astype(F32)
        for j in range(1, 8):
            total = total + ref[j].astype(F32)
        return total

    for k in ORDER7:
        p2[k].wait_recv()
    after = (xz[z].astype(F32) + sum8(rz)).astype(BF)
    imgs[c] = after
    e1 = rcopy(imgs.at[c], imgs.at[c], sbs.at[1], sbr.at[1], sib)
    e1.start()
    e1.wait_recv()
    first, second = imgs[0], imgs[1]
    left = iota((FEAT, 128), 1) < 64
    stack = []
    for t in range(2):
        a, b = first[:, 128 * t : 128 * t + 128], second[:, 128 * t : 128 * t + 128]
        stack.append(jnp.where(left, a, pltpu.roll(b, 64, 1)))
        stack.append(jnp.where(left, pltpu.roll(a, 64, 1), b))
    grouped = jnp.concatenate(stack, axis=0)
    p3[...] = dg(wm[...], grouped, 1, 0).astype(BF).reshape(8, HALF, 128)
    c3 = z_scatter(2, p3, r3)

    x_done(2)
    b_done(2)

    def build_c(row, carry):
        wc[pl.ds(pl.multiple_of(FEAT * row, 16), FEAT), :] = jnp.concatenate(pieces(2, row), axis=0)
        return carry

    lax.fori_loop(0, NY, build_c, 0)

    for k in ORDER7:
        c3[k].wait_recv()
    mt[y] = sum8(r3).astype(BF)
    c4 = {k: rcopy(mt.at[y], mt.at[y], y4s.at[k], y4r.at[k], ypeer(k)) for k in ORDER7}
    for k in ORDER7:
        c4[k].start()
    for k in ORDER7:
        c4[k].wait_recv()
    tokens = jnp.concatenate([mt[j] for j in range(8)], axis=1)

    def routed(t):
        return dg(tokens, hot[t], 1, 1).astype(BF)

    c5 = {}
    for k in ORDER3:
        to = (x + k) % NX
        route_s[k] = routed(to)
        c5[k] = rcopy(route_s.at[k], route_r.at[k], x5s.at[k], x5r.at[k], xpeer(k))
        c5[k].start()
    image = routed(x).astype(F32)
    text_cp.wait_recv()
    my_text = txt[0, c].astype(F32) + txt[1, 0].astype(F32)
    for k in ORDER3:
        c5[k].wait_recv()
        image = image + route_r[k].astype(F32)
    dec_in = jnp.where(seen[0:1, :] > 0.5, image, my_text)
    dz[z, c] = dec_in.astype(BF)

    p6 = z_gather(3, dz.at[z, c])

    def b6(k):
        ref = dz.at[(z + NZ - k) % NZ, c]
        return rcopy(ref, ref, b6s.at[k], b6r.at[k], sib)

    b6(0).start()
    for k in ORDER7:
        p6[k].wait_recv()
        b6(k).start()
    for k in range(8):
        b6(k).wait_recv()
    xd = dz[...].reshape(1280, ROWS).astype(F32)
    power = jnp.sum(xd * xd, axis=0, keepdims=True) * (1.0 / 1280.0)
    g1 = gains[1]
    gain = jnp.concatenate([g1, g1, g1[:, :64]], axis=1)
    normed = (xd * lax.rsqrt(power + EPS) * gain).astype(BF)
    proj = dg(wc[:, :512], normed, 0, 0).astype(BF)
    proj = jnp.where(c == 0, proj[:240], proj[240:480])
    qb[y] = proj[:80]
    kv[x] = proj[80:240]

    def q_copy(k):
        ref = qb.at[y]
        return rcopy(ref, ref, q7s.at[k], q7r.at[k], dev((y + NY - k) % NY, x, c, z))

    c7 = {k: rcopy(kv.at[x], kv.at[x], k7s.at[k], k7r.at[k], xpeer(k)) for k in ORDER3}
    for k in ORDER3:
        c7[k].start()
    for k in range(1, 8):

        @pl.when(y >= k)
        def _():
            q_copy(k).start()

    for k in ORDER3:
        c7[k].wait_recv()
    for t in range(NX):
        kt[t] = kv[t, :80].astype(F32).T.astype(BF)

    def o_copy(k):
        return rcopy(ob.at[k], orx.at[y], o8s.at[k], o8r.at[k], dev((y + k) % NY, x, c, z))

    def q_block(k, carry):
        @pl.when(k > 0)
        def _():
            q_copy(k).wait_recv()

        q = qb[y + k]
        limit = 1280 * k + ROWS * x + iota((ROWS, ROWS), 1)
        best = jnp.full((1, ROWS), -jnp.inf, F32)
        for t in range(NX):
            s = dg(kt[t], q, 1, 0) * SCALE
            s = jnp.where(iota((ROWS, ROWS), 0) + ROWS * t <= limit, s, -jnp.inf)
            best = jnp.maximum(best, jnp.max(s, axis=0, keepdims=True))
            sc[t] = s
        total = jnp.zeros((1, ROWS), F32)
        o = jnp.zeros((80, ROWS), F32)
        for t in range(NX):
            p = jnp.exp(sc[t] - best)
            total = total + jnp.sum(p, axis=0, keepdims=True)
            o = o + dg(kv[t, 80:], p.astype(BF), 1, 0)
        ob[k, :80] = (o / total).astype(BF)
        lse = best + jnp.log(total)
        hi = lse.astype(BF).astype(F32)
        mid = (lse - hi).astype(BF).astype(F32)
        low = lse - hi - mid
        at = iota((8, ROWS), 0)
        rows = jnp.where(at == 0, hi, jnp.where(at == 1, mid, jnp.where(at == 2, low, 0.0)))
        ob[k, 80:] = rows.astype(BF)

        @pl.when(k > 0)
        def _():
            o_copy(k).start()

        return carry

    lax.fori_loop(0, NY - y, q_block, 0)
    orx[y] = ob[0]
    for k in range(1, 8):

        @pl.when(y >= k)
        def _():
            rcopy(ob.at[k], orx.at[y - k], o8s.at[k], o8r.at[k], ypeer(0 - k)).wait_recv()

    def lse_of(j):
        return jnp.sum(orx[j, 80:].astype(F32), axis=0, keepdims=True)

    peak = lax.fori_loop(0, y + 1, lambda j, m: jnp.maximum(m, lse_of(j)), jnp.full((1, ROWS), -jnp.inf, F32))

    def merge_part(j, carry):
        o, total = carry
        share = jnp.exp(lse_of(j) - peak)
        return o + orx[j, :80].astype(F32) * share, total + share

    o, total = lax.fori_loop(
        0, y + 1, merge_part, (jnp.zeros((80, ROWS), F32), jnp.zeros((1, ROWS), F32))
    )
    attd[c] = (o / total).astype(BF)
    e2 = rcopy(attd.at[c], attd.at[c], sbs.at[2], sbr.at[2], sib)
    e2.start()
    e2.wait_recv()
    both = jnp.concatenate([jnp.zeros((96, ROWS), BF), attd[0], attd[1]], axis=0)
    for j in range(8):
        rows = wc[pl.ds(pl.multiple_of(FEAT * j + HALF * c, 16), HALF), 384:640]
        p9[j] = dg(rows, both, 1, 0).astype(BF)
    c9 = z_scatter(4, p9, r9)
    for cps in (p1, p2, c3, c4, p6):
        for k in ORDER7:
            cps[k].wait_send()
    for cps in (c5, c7):
        for k in ORDER3:
            cps[k].wait_send()
    for g in range(3):
        w_sent(g)
    for k in range(8):
        b6(k).wait_send()
    for k in range(1, 8):

        @pl.when(y >= k)
        def _():
            q_copy(k).wait_send()

        @pl.when(y + k < NY)
        def _():
            o_copy(k).wait_send()

    for k in ORDER7:
        c9[k].wait_recv()
    fin[c] = (dz[z, c].astype(F32) + sum8(r9)).astype(BF)
    e3 = rcopy(fin.at[c], fin.at[c], sbs.at[3], sbr.at[3], sib)
    e3.start()
    e3.wait_recv()
    out_ref[...] = dg(place, jnp.concatenate([fin[0], fin[1]], axis=0), 1, 1).astype(BF)

    for k in ORDER7:
        c9[k].wait_send()
    for cp in (text_cp, e1, e2, e3):
        cp.wait_send()


def shards(
    patches,
    grid,
    vit_gain,
    vit_qkv,
    vit_out,
    merge_weight,
    text_embeds,
    prompt_pos,
    dec_gain,
    dec_qkv,
    dec_out,
):
    vm = pl.BlockSpec(memory_space=pltpu.VMEM)
    dma = pltpu.SemaphoreType.DMA
    scratch = [
        pltpu.VMEM((3, 2, NX, NY, 20, 640), BF),
        pltpu.VMEM((1280, 640), BF),
        pltpu.VMEM((640, 640), BF),
        pltpu.VMEM((1280, 640), BF),
        pltpu.VMEM((2, 1280, 128), F32),
        pltpu.VMEM((8, FEAT, 256), BF),
        pltpu.VMEM((8, FEAT, 256), BF),
        pltpu.VMEM((8, FEAT, 256), BF),
        pltpu.VMEM((256, 256), BF),
        pltpu.VMEM((2, FEAT, 256), BF),
        pltpu.VMEM((8, HALF, 128), BF),
        pltpu.VMEM((8, HALF, 128), BF),
        pltpu.VMEM((8, HALF, 128), BF),
        pltpu.VMEM((NX, ROWS, 1024), BF),
        pltpu.VMEM((16, ROWS), F32),
        pltpu.VMEM((2, 2, HALF, ROWS), BF),
        pltpu.VMEM((NX, HALF, ROWS), BF),
        pltpu.VMEM((NX, HALF, ROWS), BF),
        pltpu.VMEM((8, 2, HALF, ROWS), BF),
        pltpu.VMEM((NX, 160, ROWS), BF),
        pltpu.VMEM((NX, ROWS, 80), BF),
        pltpu.VMEM((8, 80, ROWS), BF),
        pltpu.VMEM((NX, ROWS, ROWS), F32),
        pltpu.VMEM((8, 88, ROWS), BF),
        pltpu.VMEM((8, 88, ROWS), BF),
        pltpu.VMEM((2, 80, ROWS), BF),
        pltpu.VMEM((8, HALF, ROWS), BF),
        pltpu.VMEM((8, HALF, ROWS), BF),
        pltpu.VMEM((2, HALF, ROWS), BF),
    ]
    sems = []
    for shape in ((5, 8), (3, 8), (3, 4), (3, 4), (8,), (4,), (8,), (8,), (4,), (8,), (4,)):
        sems += [dma(shape), dma(shape)]
    return pl.pallas_call(
        kernel,
        out_shape=jax.ShapeDtypeStruct((160, 160), BF),
        in_specs=[pl.BlockSpec(memory_space=pltpu.SMEM)] + [vm] * 10,
        out_specs=vm,
        scratch_shapes=scratch + sems,
        compiler_params=pltpu.CompilerParams(
            collective_id=0, has_side_effects=True, vmem_limit_bytes=60 << 20
        ),
        name="layer",
    )(
        grid,
        patches[0].T,
        vit_gain.reshape(10, 128),
        vit_qkv,
        vit_out.T,
        merge_weight.transpose(2, 0, 1),
        text_embeds,
        prompt_pos,
        dec_gain.reshape(10, 128),
        dec_qkv,
        dec_out.T,
    )


def solution(mesh):
    placed = (
        P("wide", None, "narrow"),
        P("wide", None),
        P(),
        P("wide", "narrow"),
        P("narrow", "wide"),
        P(None, "narrow", "wide"),
        P("wide", "narrow"),
        P(),
        P(),
        P("wide", "narrow"),
        P("narrow", "wide"),
    )
    return jax.shard_map(
        shards, mesh=mesh, in_specs=placed, out_specs=P("wide", "narrow"), check_vma=False
    )
```
